32 devices in a mesh: gx: 8 (over z, x), gy: 4 (over y, core).
Axes of the slice: x: 2, y: 2, z: 4, core: 2. Of those that a mesh axis runs over, the one named last changes fastest.
Arguments:
- features: bfloat16 [32, 8192], P(None, ('gx', 'gy')), may hold values from -6 to 6
- offsets: bfloat16 [3, 8192], P(None, ('gx', 'gy')), may hold values from 0 to 16
- point_cell: int32 [8192], P(('gx', 'gy')), may hold values from 0 to 31
- tile_owner: int32 [64, 4], P(('gx', 'gy')), may hold values from 0 to 3, all different within a row; in each aligned block of 2 rows (0 to 1, 2 to 3, ...) at most 2 rows name the same one
- tile_local: int32 [64, 4], P(('gx', 'gy')), may hold values from 0 to 31
- live_count: int32 [64], P(('gx', 'gy')), may hold values from 1 to 4
- w_first: bfloat16 [64, 3], replicated, may hold values from -3.5 to 3.5
- b_first: float32 [64], replicated, may hold values from -3 to 3
- w_second: bfloat16 [64, 64], replicated, may hold values from -0.75 to 0.75
- b_second: float32 [64], replicated, may hold values from -3 to 3
- w_third: bfloat16 [32, 64], replicated, may hold values from -0.75 to 0.75
- w_point: bfloat16 [32, 32], replicated, may hold values from -1 to 1
- b_point: float32 [32], replicated, may hold values from -3 to 3
- w_modes: bfloat16 [32, 32, 32, 2, 32, 32], P(None, 'gx', 'gy'), may hold values from -3 to 3
Outputs:
- latent_out: float32 [32, 32, 32, 128], P('gx', 'gy')
The draws below stay inside these ranges and needn't reach their ends.
Inputs may be any that keep to these rules, and one draw needn't show every extreme that they name: `tile_owner`: each row names 4 different owners; among the rows of one device no owner is named by more than 2 rows.
All inputs are finite; a program needn't handle non-finite values.
Results may differ from the reference program's by a relative error of at most 0.0015.
Values may be sent and summed in bfloat16 or wider, within the bound.
A program may use at most 64 MiB of HBM per device.

```python
import math
import jax
import jax.numpy as jnp
import numpy as np
from jax import lax

C = 32
HID = 64
M = 32
NZ = 128
CX = 4
CY = 8
SPAN = 16
PB = 128
BLK_DEV = 2
LIST = 4
CAP = 2
NX = 32
NY = 32
BLOCKS = 64
POINTS = 8192
COARSE = 32
N_GY = 4
DEVICES = 32


def draw_live_count(key, part):
    key_rows = jax.random.fold_in(key, 11)
    key_slots = jax.random.fold_in(key, 12)
    density = jax.random.randint(key_rows, (DEVICES, 1), 2, LIST + 1)
    lowest = (density + 1) // 2
    raw_draw = jax.random.randint(key_slots, (DEVICES, BLK_DEV), 0, 1 << 20)
    counts = lowest + raw_draw % (density - lowest + 1)
    return counts.reshape(BLOCKS).astype(jnp.int32)


def plant(array, key, smallest, high):
    place = [jax.random.randint(jax.random.fold_in(key, axis), (), 0, length) for axis, length in enumerate(array.shape)]
    widest = array.shape.index(max(array.shape))
    neighbour = place[:widest] + [(place[widest] + 1) % array.shape[widest]] + place[widest + 1:]
    return array.at[tuple(place)].set(smallest).at[tuple(neighbour)].set(high)


def level_of(key, dims, split, least, high):
    factor_of = 1.0
    for dim, shards_of in split:
        draws = jax.random.uniform(jax.random.fold_in(jax.random.fold_in(key, 6), dim), (shards_of,), jnp.float32, least / len(split), high / len(split))
        factor_of = factor_of * jnp.repeat(jnp.exp(draws), dims[dim] // shards_of).reshape((-1,) + (1,) * (len(dims) - 1 - dim))
    return factor_of


def routed_block(key, own, number, rows, amount, top, reach, slope):
    sequence = jax.random.permutation(key, amount)
    heavy_load, ordinary = portions_of(amount, rows * top, reach, slope, True), portions_of(amount, rows * top, reach, slope, False)
    places = jnp.arange(amount)

    def named(tallies, rotation):
        used = int((tallies > 0).sum())
        fixed = max(1, used // 4)
        passed = fixed + (places - fixed + rotation * (used - fixed)) % max(1, amount - fixed)
        return jnp.zeros((amount,), jnp.int32).at[sequence[jnp.where(places < fixed, places, passed)]].set(jnp.asarray(tallies, jnp.int32))

    tallies = jnp.where(number % 4 == 0, named(heavy_load, number // 4), named(ordinary, number - number // 4 - 1))
    mixed = jax.random.permutation(jax.random.fold_in(own, 3), amount)
    giver, taker = mixed[0:amount // 2 * 2:2], mixed[1:amount // 2 * 2:2]
    slack = jnp.minimum(tallies[giver] - 1, reach - tallies[taker]) // 2
    slack = jnp.where((giver == sequence[0]) | (taker == sequence[0]) | (tallies[taker] == 0), 0, jnp.maximum(slack, 0))
    passed = jax.random.randint(jax.random.fold_in(own, 4), (amount // 2,), 0, 1 << 20) % (slack + 1)
    tallies = tallies.at[giver].add(-passed).at[taker].add(passed)
    items = jnp.searchsorted(jnp.cumsum(tallies), jnp.arange(rows * top), side="right").astype(jnp.int32)
    table = items.reshape(top, rows).T
    table = table[jax.random.permutation(jax.random.fold_in(own, 1), rows)]
    rotation = jax.random.randint(jax.random.fold_in(own, 2), (rows, 1), 0, top)
    return jnp.take_along_axis(table, (jnp.arange(top)[None, :] + rotation) % top, axis=1)


def portions_of(count, total, reach, lean, full):
    portions = [(1 << 20) // math.isqrt(standing ** lean) + 1 for standing in range(1, count + 1)]
    largest = reach if full else min(reach, max(-(-total // count), total * portions[0] // sum(portions)))
    least = 1 if total - largest >= count - 1 else 0
    given, spare = [largest] + [least] * (count - 1), total - largest - least * (count - 1)
    while spare > 0:
        movable = [i for i in range(1, count) if given[i] < largest] or [i for i in range(1, count) if given[i] < reach]
        pool, budget = sum([portions[i] for i in movable]), spare
        for i in movable:
            extra = min(reach - given[i], max(1, budget * portions[i] // pool), spare)
            given[i] = given[i] + extra
            spare = spare - extra
    return np.array(given)


def bell_draw(stream_key, shape, spread, limit, pieces=(), kind=jnp.bfloat16):
    result = spread * jax.random.normal(stream_key, shape, jnp.float32)
    if pieces:
        result = result * level_of(stream_key, shape, pieces, -0.22, 0.18)
    return jnp.clip(result, -limit, limit).astype(kind)


def setup_inputs(seed: int = 0) -> dict:
    key_list = jax.random.split(jax.random.key(seed), 15)
    features = bell_draw(key_list[0], (C, POINTS), 1.0, 6.0, ((1, 32),))
    offsets = jnp.clip(16.0 * jax.random.uniform(key_list[1], (3, POINTS), jnp.float32) ** level_of(key_list[1], (3, POINTS), ((1, 32),), -0.2, 0.2), 0.0, 16.0).astype(jnp.bfloat16)
    point_cell = plant(jax.random.randint(key_list[2], (POINTS,), 0, COARSE), jax.random.fold_in(key_list[2], 1), 0, COARSE - 1).astype(jnp.int32)
    tile_owner_keys = jax.random.split(jax.random.fold_in(key_list[3], 1), BLOCKS // BLK_DEV)
    tile_owner_turns = jax.random.permutation(jax.random.fold_in(key_list[3], 3), BLOCKS // BLK_DEV)
    tile_owner = jax.vmap(lambda own, number: routed_block(jax.random.fold_in(key_list[3], 2), own, number, BLK_DEV, N_GY, LIST, CAP, 0))(tile_owner_keys, tile_owner_turns).reshape((BLOCKS, LIST))
    tile_local = plant(jax.random.randint(key_list[4], (BLOCKS, LIST), 0, CX * CY), jax.random.fold_in(key_list[4], 1), 0, (CX * CY) - 1).astype(jnp.int32)
    live_count = draw_live_count(jax.random.fold_in(key_list[14], 71), 0)
    w_first = bell_draw(key_list[6], (HID, 3), 3 ** -0.5, 3.5)
    b_first = bell_draw(key_list[7], (HID,), 0.5, 3.0, (), jnp.float32)
    w_second = bell_draw(key_list[8], (HID, HID), HID ** -0.5, 0.75)
    b_second = bell_draw(key_list[9], (HID,), 0.5, 3.0, (), jnp.float32)
    w_third = bell_draw(key_list[10], (C, HID), HID ** -0.5, 0.75)
    w_point = bell_draw(key_list[11], (C, C), C ** -0.5, 1.0)
    b_point = bell_draw(key_list[12], (C,), 0.5, 3.0, (), jnp.float32)
    w_modes = bell_draw(key_list[13], (M, M, M, 2, C, C), 0.5, 3.0, ((1, 8), (2, 4)))
    return {"features": features, "offsets": offsets, "point_cell": point_cell, "tile_owner": tile_owner, "tile_local": tile_local, "live_count": live_count, "w_first": w_first, "b_first": b_first, "w_second": w_second, "b_second": b_second, "w_third": w_third, "w_point": w_point, "b_point": b_point, "w_modes": w_modes}


def phase_tables(length, modes, two_sided):
    orders = jnp.arange(modes, dtype=jnp.int32)
    if two_sided:
        frequency = jnp.where(orders < modes // 2, orders, length - modes + orders)
    else:
        frequency = orders
    places = jnp.arange(length, dtype=jnp.int32)
    turns = places[:, None] * frequency[None, :] % length
    angles = turns.astype(jnp.float32) * (2.0 * math.pi / length)
    return (jnp.cos(angles), jnp.sin(angles))

def complex_table(length, modes, direction):
    cosine, sine = phase_tables(length, modes, True)
    return jnp.stack([jnp.stack([cosine, direction * sine], -1), jnp.stack([-direction * sine, cosine], -1)], 1)

def inverse_table(length, modes):
    return jnp.transpose(complex_table(length, modes, 1.0), (2, 1, 0, 3))

def real_tables(length, modes, scale):
    cosine, sine = phase_tables(length, modes, False)
    forward = jnp.stack([cosine, -sine], -1) * scale
    inverse = jnp.stack([cosine.T, -sine.T], 1) * scale
    return (forward, inverse)

def pair_sum(block_feats, block_offsets, cell_ids, cell_x, cell_y, weights, grid_dims):
    w_first, b_first, w_second, b_second, w_third = weights
    coarse_y, coarse_z, depth = grid_dims
    along_x = cell_ids // (coarse_y * coarse_z)
    along_y = cell_ids // coarse_z % coarse_y
    along_z = cell_ids % coarse_z
    places = jnp.stack([along_x, along_y, along_z]).astype(jnp.float32) * SPAN + block_offsets.astype(jnp.float32)
    column = jnp.arange(depth, dtype=jnp.int32).astype(jnp.float32)
    centres = jnp.stack([jnp.zeros_like(column) + cell_x.astype(jnp.float32), jnp.zeros_like(column) + cell_y.astype(jnp.float32), column])
    layer_one = w_first.astype(jnp.float32)
    cell_side = layer_one[:, 0:1] * centres[0:1] + layer_one[:, 1:2] * centres[1:2] + layer_one[:, 2:3] * centres[2:3]
    point_side = layer_one[:, 0:1] * places[0:1] + layer_one[:, 1:2] * places[1:2] + layer_one[:, 2:3] * places[2:3]
    inputs = cell_side[:, :, None] - point_side[:, None, :] + b_first[:, None, None]
    hidden = jnp.sin(inputs).astype(jnp.bfloat16).reshape(w_first.shape[0], -1)
    second = jnp.dot(w_second, hidden, preferred_element_type=jnp.float32) + b_second[:, None]
    second = jax.nn.gelu(second).astype(jnp.bfloat16)
    kernel = jnp.dot(w_third, second, preferred_element_type=jnp.float32).reshape(w_third.shape[0], depth, -1)
    return lax.optimization_barrier(jnp.sum(kernel * block_feats.astype(jnp.float32)[:, None, :], axis=2)) / math.sqrt(block_feats.shape[1])

def mix_modes(spectrum, w_modes):
    weights = w_modes.astype(jnp.float32)
    real_in = spectrum[..., 0, :]
    imag_in = spectrum[..., 1, :]
    real_w = weights[..., 0, :, :]
    imag_w = weights[..., 1, :, :]
    form = 'kpqi,kpqio->kpqo'
    best = lax.Precision.HIGHEST
    real_out = jnp.einsum(form, real_in, real_w, precision=best) - jnp.einsum(form, imag_in, imag_w, precision=best)
    imag_out = jnp.einsum(form, real_in, imag_w, precision=best) + jnp.einsum(form, imag_in, real_w, precision=best)
    return jnp.stack([real_out, imag_out], 3)

def fourier_layer(latent, w_point, b_point, w_modes):
    size_x, size_y, channels, depth = latent.shape
    modes = w_modes.shape[0]
    best = lax.Precision.HIGHEST
    scale = 1.0 / math.sqrt(size_x * size_y * depth)
    forward_z, inverse_z = real_tables(depth, modes, scale)
    along_z = jnp.einsum('xycz,zks->xyksc', latent, forward_z, precision=best)
    along_y = jnp.einsum('xyqrc,yrks->xkqsc', along_z, complex_table(size_y, modes, -1.0), precision=best)
    spectrum = jnp.einsum('xpqrc,xrks->kpqsc', along_y, complex_table(size_x, modes, -1.0), precision=best)
    mixed = mix_modes(spectrum, w_modes)
    back_x = jnp.einsum('kpqrc,krxs->xpqsc', mixed, inverse_table(size_x, modes), precision=best)
    back_y = jnp.einsum('xpqrc,prys->xyqsc', back_x, inverse_table(size_y, modes), precision=best)
    spectral = jnp.einsum('xyqrc,qrz->xycz', back_y, inverse_z, precision=best)
    pointwise = jnp.einsum('xycz,co->xyoz', latent, w_point.astype(jnp.float32), precision=best)
    return jax.nn.gelu(spectral + pointwise + b_point[:, None])

def reference(features, offsets, point_cell, tile_owner, tile_local, live_count, w_first, b_first, w_second, b_second, w_third, w_point, b_point, w_modes):
    weights = (w_first, b_first, w_second, b_second, w_third)
    grid_dims = (NY // SPAN, NZ // SPAN, NZ)
    block_feats = features.reshape(C, BLOCKS, PB).transpose(1, 0, 2)
    block_offsets = offsets.reshape(3, BLOCKS, PB).transpose(1, 0, 2)
    block_cells = point_cell.reshape(BLOCKS, PB)
    pair_ids = jnp.arange(BLOCKS * LIST, dtype=jnp.int32)
    block_ids = pair_ids // LIST
    slot_ids = pair_ids % LIST
    row_ids = block_ids // (BLK_DEV * N_GY)
    owners = tile_owner.reshape(-1)
    tile_slot = tile_local.reshape(-1)
    cell_x = CX * row_ids + tile_slot // CY
    cell_y = CY * owners + tile_slot % CY
    is_live = slot_ids < live_count[block_ids]

    def one_pair(pair_index):
        block_now = block_ids[pair_index]
        return lax.cond(is_live[pair_index], lambda: pair_sum(block_feats[block_now], block_offsets[block_now], block_cells[block_now], cell_x[pair_index], cell_y[pair_index], weights, grid_dims), lambda: jnp.zeros((C, NZ), jnp.float32))
    contribs = lax.map(one_pair, pair_ids)
    grid = jnp.zeros((NX * NY, C, NZ), jnp.float32).at[cell_x * NY + cell_y].add(contribs)
    latent = grid.reshape(NX, NY, C, NZ)
    return fourier_layer(latent, w_point, b_point, w_modes)
```

```python
import math

import jax
import numpy as np
import jax.numpy as jnp
from jax import lax
from jax.experimental import pallas as pl
from jax.experimental.pallas import tpu as pltpu
from jax.sharding import PartitionSpec as P

NZ = 128
CX = 4
CY = 8
SPAN = 16
PB = 128
LANES = 128

GROUP = 4
UNROLL = 8

LINEAR = 2.0 * math.sqrt(2.0 / math.pi)
CUBIC = 4.0 * 0.044715 * LINEAR

f32 = jnp.float32
bf16 = jnp.bfloat16


def halves(value):
    high = value.astype(bf16)
    return high, (value - high.astype(f32)).astype(bf16)


def split_rows(value):
    high, low = halves(value)
    return jnp.concatenate([high, low, high], 0)


def split_table(table):
    table = np.asarray(table, np.float32)
    high = table.astype(jnp.bfloat16)
    low = (table - high.astype(np.float32)).astype(jnp.bfloat16)
    return np.concatenate([high, high, low], 1)


def matmul(left, right):
    return jnp.dot(left, right, preferred_element_type=f32)


def tables(cols_x, cols_y, modes):
    size_x, size_y = CX * cols_x, CY * cols_y
    own_p, own_q = modes // cols_x, modes // cols_y
    scale = 1.0 / math.sqrt(size_x * size_y * NZ)

    def frequencies(length):
        order = np.arange(modes)
        return np.where(order < modes // 2, order, length - modes + order)

    def turn(angle):
        cosine, sine = np.cos(angle), np.sin(angle)
        return np.array([[cosine, -sine], [sine, cosine]])

    z_turns = 2 * np.pi * (np.outer(np.arange(modes), np.arange(NZ)) % NZ) / NZ
    waves = np.stack([np.cos(z_turns), -np.sin(z_turns)], 0) * scale
    waves = waves.reshape(2, cols_y, own_q, NZ)
    z_table = waves.transpose(2, 0, 1, 3).reshape(-1, NZ)
    inverse = waves.transpose(2, 1, 0, 3).reshape(-1, NZ)
    inverse = np.asarray(inverse, np.float32)
    high = inverse.astype(jnp.bfloat16)
    low = (inverse - high.astype(np.float32)).astype(jnp.bfloat16)
    inverse = np.concatenate([high, high, low], 0)
    x_turns = 2 * np.pi * (np.outer(frequencies(size_x), np.arange(size_x)) % size_x) / size_x
    backward = turn(x_turns).reshape(2, 2, modes // 4, 4, cols_x, CX)
    backward = np.einsum("srgkdx,pP->dsPxpgrk", backward, np.eye(own_p))
    backward = backward.reshape(-1, modes * 2 * own_p)
    y_turns = 2 * np.pi * (np.outer(frequencies(size_y), np.arange(size_y)) % size_y) / size_y
    lift = turn(y_turns).reshape(2, 2, cols_x, own_p, cols_y, CY)
    lift = np.einsum("srepdy,xX->dsxyerpX", lift, np.eye(CX))
    lift = lift.reshape(2 * CX * size_y, -1)
    return split_table(z_table), split_table(backward), split_table(lift), inverse


def encoder_kernel(
    owner_ref,
    local_ref,
    live_ref,
    features_ref,
    offsets_ref,
    cells_ref,
    turned_first_ref,
    b_first_ref,
    w_second_ref,
    b_second_ref,
    w_third_ref,
    z_table_ref,
    backward_ref,
    lift_ref,
    modes_ref,
    codes_ref,
    held_ref,
    back_ref,
    weights,
    cell_sin,
    cell_cos,
    point_sin,
    point_cos,
    spread_two,
    spread_three,
    feats,
    second,
    sums,
    code_sent,
    code_got,
    sent_a,
    got_a,
    raw_sent,
    phases,
    splits,
    spectra,
    mixed,
    sent_d,
    got_d,
    sent_e,
    load_sem,
    sends,
    recvs,
):
    cols_x, cols_y = lax.axis_size("gx"), lax.axis_size("gy")
    mine_x, mine_y = lax.axis_index("gx"), lax.axis_index("gy")
    count = cols_x * cols_y
    me = mine_x * cols_y + mine_y
    blocks, listed = owner_ref.shape
    hid = w_second_ref.shape[0]
    channels = w_third_ref.shape[0]
    wide = GROUP * hid
    two = 2 * hid
    quarter = PB // GROUP
    size_x, size_y = CX * cols_x, CY * cols_y
    load = pltpu.make_async_copy(modes_ref, weights, load_sem)
    load.start()

    def everyone(body):
        if count <= 32:
            for step in range(1, count):
                body(step)
        else:
            pl.loop(1, count)(body)

    def place(step):
        other = lax.rem(me + step, count)
        return other // cols_y, lax.rem(other, cols_y)

    barrier = pltpu.get_barrier_semaphore()

    def greet(step):
        x, y = place(step)
        pl.semaphore_signal(barrier, inc=1, device_id={"gx": x, "gy": y})

    everyone(greet)

    turned_two = (w_second_ref[...].astype(f32).T * 0.5).astype(bf16)
    turned_three = w_third_ref[...].astype(f32).T
    spread_two[...] = jnp.zeros_like(spread_two)
    spread_three[...] = jnp.zeros_like(spread_three)
    for part in range(GROUP):
        rows = slice(part * hid, (part + 1) * hid)
        spread_two[rows, rows] = turned_two
    bias = jnp.concatenate([b_second_ref[...] * 0.5] * GROUP, 1)
    wide_three = jnp.concatenate([turned_three] * GROUP, 1)
    coarse_y, coarse_z = size_y // SPAN, NZ // SPAN
    cells = cells_ref[...]
    coarse = jnp.concatenate(
        [cells // (coarse_y * coarse_z), cells // coarse_z % coarse_y, cells % coarse_z], 0
    )
    places = coarse.astype(f32) * SPAN + offsets_ref[...].astype(f32)
    places = jnp.concatenate([places, jnp.zeros((5, places.shape[1]), f32)], 0)
    turned_first = turned_first_ref[...].astype(f32)
    double_first = jnp.concatenate([turned_first, turned_first], 1)
    features = features_ref[...].astype(f32)

    steps = lax.broadcasted_iota(jnp.int32, (24, two), 0)
    steps = jnp.where(steps < 16, steps * 8, steps - 16).astype(f32)
    steps = steps * double_first[2:3]
    cosine, sine = jnp.cos(steps), jnp.sin(steps)
    cos_fine, sin_fine = cosine[16:24], sine[16:24]
    bases = []
    for block in range(blocks):
        for slot in range(listed):
            tile = local_ref[block, slot]
            cell_x = (CX * mine_x + tile // CY).astype(f32)
            cell_y = (CY * owner_ref[block, slot] + tile % CY).astype(f32)
            bases.append(
                turned_first[0:1] * cell_x + turned_first[1:2] * cell_y + b_first_ref[...]
            )
    base = jnp.concatenate(bases, 0)
    base = jnp.concatenate([base, base], 1)
    base_sin, base_cos = jnp.sin(base), jnp.cos(base)
    code_lane = lax.broadcasted_iota(jnp.int32, (1, LANES), 1)
    code_rows = []
    for block in range(blocks):
        row = jnp.zeros((1, LANES), jnp.int32)
        for slot in range(listed):
            code = owner_ref[block, slot] * (CX * CY) + local_ref[block, slot]
            row = jnp.where(code_lane % listed == slot, code, row)
        code_rows.append(row)
    for block in range(blocks):
        row = jnp.full((1, LANES), -1, jnp.int32)
        for slot in range(listed):
            alive = jnp.where(slot < live_ref[block], local_ref[block, slot], -1)
            row = jnp.where(code_lane == owner_ref[block, slot], alive, row)
        code_rows.append(row)
    code_rows.append(jnp.zeros((8 - 2 * blocks, LANES), jnp.int32))
    code_sent[...] = jnp.concatenate(code_rows, 0)

    lane = lax.broadcasted_iota(jnp.int32, (quarter, two), 1)

    def pairs(block):
        here = slice(block * PB, (block + 1) * PB)
        for slot in range(listed):
            item = block * listed + slot
            b_sin, b_cos = base_sin[item : item + 1], base_cos[item : item + 1]
            near_sin = sin_fine * b_cos + cos_fine * b_sin
            near_cos = cos_fine * b_cos - sin_fine * b_sin
            for step in range(NZ // 8):
                rows = slice(slot * NZ + step * 8, slot * NZ + step * 8 + 8)
                far_cos, far_sin = cosine[step : step + 1], sine[step : step + 1]
                cell_sin[rows, :] = far_cos * near_sin + far_sin * near_cos
                cell_cos[rows, :] = far_cos * near_cos - far_sin * near_sin
        spots = places[:, here].T
        side = (
            double_first[0:1] * spots[:, 0:1]
            + double_first[1:2] * spots[:, 1:2]
            + double_first[2:3] * spots[:, 2:3]
        )
        side_cos, side_sin = jnp.cos(side), jnp.sin(side)
        for half in range(GROUP // 2):
            low = slice(2 * half * quarter, (2 * half + 1) * quarter)
            up = slice((2 * half + 1) * quarter, (2 * half + 2) * quarter)
            cols = slice(half * two, (half + 1) * two)
            point_cos[:, cols] = jnp.where(lane < hid, side_cos[low], side_cos[up])
            point_sin[:, cols] = jnp.where(lane < hid, side_sin[low], side_sin[up])
        turned = features[:, here].T
        feats[...] = jnp.concatenate(
            [turned[j * quarter : (j + 1) * quarter] for j in range(GROUP)], 1
        )
        sums[...] = jnp.zeros_like(sums)

        @pl.loop(0, quarter // UNROLL)
        def _(step):
            for inner in range(UNROLL):
                weigh = wide_three * feats[pl.ds(step * UNROLL + inner, 1), :]
                high, rest = halves(weigh)
                for part in range(GROUP):
                    rows = slice(inner * wide + part * hid, inner * wide + (part + 1) * hid)
                    cols = slice(part * channels, (part + 1) * channels)
                    spread_three[rows, part * channels : (part + 1) * channels] = high[:, cols]
                    spread_three[
                        rows, LANES + part * channels : LANES + (part + 1) * channels
                    ] = rest[:, cols]
            for slot in range(listed):
                rows = slice(slot * NZ, (slot + 1) * NZ)
                for inner in range(UNROLL):
                    group = step * UNROLL + inner
                    p_cos, p_sin = point_cos[pl.ds(group, 1), :], point_sin[pl.ds(group, 1), :]
                    c_sin, c_cos = cell_sin[rows, :], cell_cos[rows, :]
                    hidden = []
                    for half in range(GROUP // 2):
                        cols = slice(half * two, (half + 1) * two)
                        value = c_sin * p_cos[:, cols] - c_cos * p_sin[:, cols]
                        hidden.append(value.astype(bf16))
                    y = matmul(jnp.concatenate(hidden, 1), spread_two[...]) + bias
                    bent = jnp.tanh(y * (LINEAR + CUBIC * (y * y)))
                    second[rows, inner * wide : (inner + 1) * wide] = (y + y * bent).astype(bf16)
                sums[rows, :] += matmul(second[rows, :], spread_three[...])

    own_q = sent_a.shape[3] // channels
    lane_z = lax.broadcasted_iota(jnp.int32, (NZ, LANES), 1) // channels
    lane_r = lax.broadcasted_iota(jnp.int32, (quarter, LANES), 1) // channels
    scale = 1.0 / math.sqrt(PB)

    def parcels(block):
        flat = jnp.zeros((NZ, LANES), f32)
        dense = []
        for slot in range(listed):
            rows = slice(slot * NZ, (slot + 1) * NZ)
            total = sums[rows, 0:LANES] + sums[rows, LANES:]
            total = total + pltpu.roll(total, 2 * channels, 1)
            total = total + pltpu.roll(total, channels, 1)
            total = jnp.where(slot < live_ref[block], total * scale, 0.0)
            flat = jnp.where(lane_z == slot, total, flat)
            tight = total[0:quarter]
            for part in range(1, GROUP):
                tight = jnp.where(
                    lane_r == part, total[part * quarter : (part + 1) * quarter], tight
                )
            dense.append(tight)
        modes = matmul(z_table_ref[...], split_rows(flat))
        span = 2 * cols_y
        for slot in range(listed):
            lanes = slice(slot * channels, (slot + 1) * channels)
            joined = jnp.concatenate(
                [modes[q * span : (q + 1) * span, lanes] for q in range(own_q)], 1
            )
            for part in range(2):
                sent_a[block, :, part * listed + slot, :] = joined[
                    part * cols_y : (part + 1) * cols_y
                ]
        for dest in range(cols_y):
            chosen = jnp.zeros((quarter, LANES), f32)
            for slot in range(listed):
                chosen = jnp.where(owner_ref[block, slot] == dest, dense[slot], chosen)
            raw_sent[dest, block] = chosen

    def send(source, target, stage, x, y):
        pltpu.make_async_remote_copy(
            src_ref=source,
            dst_ref=target,
            send_sem=sends.at[stage],
            recv_sem=recvs.at[stage],
            device_id={"gx": x, "gy": y},
        ).start()

    def keep(source, target, stage):
        pltpu.make_async_copy(source, target, recvs.at[stage]).start()

    def spread(block):
        def go(step):
            x, y = place(step)
            send(sent_a.at[block, y], got_a.at[block, me], block, x, y)

        everyone(go)
        keep(sent_a.at[block, mine_y], got_a.at[block, me], block)

    def arrive(target, stage):
        pltpu.make_async_copy(target, target, recvs.at[stage]).wait()

    def depart(part, stage):
        pltpu.make_async_copy(part, part, sends.at[stage]).wait()

    stage_code, stage_raw, stage_d, stage_e = blocks, blocks + 1, blocks + 2, blocks + 3

    pairs(0)
    parcels(0)
    pl.semaphore_wait(barrier, count - 1)

    def tell(step):
        x, y = place(step)
        send(code_sent, code_got.at[me], stage_code, x, y)

    everyone(tell)
    keep(code_sent, code_got.at[me], stage_code)
    spread(0)
    for block in range(1, blocks):
        pairs(block)
        parcels(block)
        spread(block)

    for step in range(1, cols_y):
        other = lax.rem(mine_y + step, cols_y)
        send(raw_sent.at[other], held_ref.at[mine_y], stage_raw, mine_x, other)
    keep(raw_sent.at[mine_y], held_ref.at[mine_y], stage_raw)

    arrive(code_got, stage_code)
    own_p = sent_d.shape[1] // (2 * CX)
    modes = own_p * cols_x
    each = 2 * listed
    depth = count * each
    column = lax.broadcasted_iota(jnp.int32, (1, depth), 1)
    source = column // each
    slots = modes * 2
    row = lax.broadcasted_iota(jnp.int32, (slots, depth), 0)
    which = (row // 8) * 4 + row % 4
    freq_x = jnp.where(which < modes // 2, which, size_x - modes + which)
    part_out = (row // 4) % 2
    part_in = (column // listed) % 2
    quarters = (part_out - part_in).astype(f32) * 0.25
    p_at = mine_x * own_p + lax.broadcasted_iota(jnp.int32, (own_p, depth), 0)
    freq_y = jnp.where(p_at < modes // 2, p_at, size_y - modes + p_at)
    owns = (
        lax.broadcasted_iota(jnp.int32, (count, depth), 1) // each
        == lax.broadcasted_iota(jnp.int32, (count, depth), 0)
    )

    def waves(turns):
        angle = (turns - jnp.floor(turns)) * (2.0 * math.pi)
        return jnp.cos(angle), jnp.sin(angle)

    for block in range(blocks):
        codes = jnp.concatenate([code_got[:, block, :].astype(f32)] * (depth // LANES), 1)
        code = jnp.sum(jnp.where(owns, codes, 0.0), axis=0, keepdims=True).astype(jnp.int32)
        tile = code % (CX * CY)
        x_at = CX * (source // cols_y) + tile // CY
        y_at = CY * (code // (CX * CY)) + tile % CY
        x_cos, x_sin = waves((freq_x * x_at).astype(f32) * (1.0 / size_x) + quarters)
        y_cos, y_sin = waves((freq_y * y_at).astype(f32) * (1.0 / size_y))
        for p in range(own_p):
            value = x_cos * y_cos[p : p + 1] - x_sin * y_sin[p : p + 1]
            high, low = halves(value)
            rows = slice(p * slots, (p + 1) * slots)
            start = block * 3 * depth
            phases[rows, start : start + depth] = high
            phases[rows, start + depth : start + 2 * depth] = high
            phases[rows, start + 2 * depth : start + 3 * depth] = low
    lanes_w = got_a.shape[3]
    for block in range(blocks):
        arrive(got_a.at[block], block)
        splits[block * 3 * depth : (block + 1) * 3 * depth, :] = split_rows(
            got_a[block].reshape(depth, lanes_w)
        )
    spectra[...] = matmul(phases[...], splits[...])

    load.wait()
    quad = 8 * channels
    row_of = lax.broadcasted_iota(jnp.int32, (8, quad), 0)
    lane_of = lax.broadcasted_iota(jnp.int32, (8, quad), 1)
    own_four = lane_of // (2 * channels) == row_of % 4
    negate = lax.broadcasted_iota(jnp.int32, (8, lanes_w), 0) < 4
    fours = modes // 4
    ahead = 4

    @pl.loop(0, own_p * fours // ahead)
    def _(outer):
        for inner in range(ahead):
            group = outer * ahead + inner
            p = group // fours
            low = (group % fours) * 4
            start = pl.multiple_of(group * 8, 8)
            plain = spectra[pl.ds(start, 8), :]
            turned = pltpu.roll(plain, 4, 0)
            turned = jnp.where(negate, -turned, turned)
            outs = []
            for q in range(own_q):
                lanes = slice(q * channels, (q + 1) * channels)
                both = jnp.concatenate([plain[:, lanes], turned[:, lanes]], 1)
                both = jnp.where(own_four, jnp.concatenate([both] * 4, 1), 0.0)
                high, rest = halves(both)
                tile = weights[pl.ds(low, 4), p, q].reshape(quad, channels)
                out = matmul(jnp.concatenate([high, rest], 0), tile)
                outs.append(out[:8] + out[8:])
            mixed[pl.ds(start, 8), :] = jnp.concatenate(outs, 1)

    along_x = matmul(backward_ref[...], split_rows(mixed[...]))
    sent_d[...] = along_x.reshape(sent_d.shape)
    for step in range(1, cols_x):
        other = lax.rem(mine_x + step, cols_x)
        send(sent_d.at[other], got_d.at[mine_x], stage_d, other, mine_y)
    keep(sent_d.at[mine_x], got_d.at[mine_x], stage_d)
    arrive(got_d, stage_d)
    along_y = matmul(lift_ref[...], split_rows(got_d[...].reshape(-1, lanes_w)))
    sent_e[...] = along_y.reshape(sent_e.shape)
    for step in range(1, cols_y):
        other = lax.rem(mine_y + step, cols_y)
        send(sent_e.at[other], back_ref.at[mine_y], stage_e, mine_x, other)
    keep(sent_e.at[mine_y], back_ref.at[mine_y], stage_e)
    codes_ref[...] = code_got[pl.ds(mine_x * cols_y, cols_y)]
    for block in range(blocks):
        depart(got_a.at[block, pl.ds(0, count - 1)], block)
    depart(code_got.at[pl.ds(0, count - 1)], stage_code)
    depart(raw_sent.at[pl.ds(0, cols_y - 1)], stage_raw)
    depart(sent_d.at[pl.ds(0, cols_x - 1)], stage_d)
    arrive(held_ref, stage_raw)
    arrive(back_ref, stage_e)
    depart(sent_e.at[pl.ds(0, cols_y - 1)], stage_e)


def encoder(
    features,
    offsets,
    point_cell,
    tile_owner,
    tile_local,
    live_count,
    w_first,
    b_first,
    w_second,
    b_second,
    w_third,
    w_modes,
    z_table,
    backward,
    lift,
):
    cols_x, cols_y = lax.axis_size("gx"), lax.axis_size("gy")
    count = cols_x * cols_y
    own_p, own_q = w_modes.shape[1:3]
    modes, channels = w_modes.shape[0], w_modes.shape[-1]
    hid = w_third.shape[1]
    blocks, listed = tile_owner.shape
    lanes = own_q * channels
    wide = GROUP * hid
    quarter = PB // GROUP
    depth = count * 2 * listed
    slots = modes * 2 * own_p
    smem = pl.BlockSpec(memory_space=pltpu.SMEM)
    vmem = pl.BlockSpec(memory_space=pltpu.VMEM)
    last = (cols_y, 2 * CX * CY, lanes)
    parcel = (cols_x, 2 * own_p * CX, lanes)
    return pl.pallas_call(
        encoder_kernel,
        out_shape=(
            jax.ShapeDtypeStruct((cols_y, 8, LANES), jnp.int32),
            jax.ShapeDtypeStruct((cols_y, blocks, quarter, LANES), f32),
            jax.ShapeDtypeStruct(last, f32),
        ),
        in_specs=[smem] * 3 + [vmem] * 11 + [pl.BlockSpec(memory_space=pl.ANY)],
        out_specs=(vmem, vmem, vmem),
        scratch_shapes=[
            pltpu.VMEM(w_modes.shape, w_modes.dtype),
            pltpu.VMEM((listed * NZ, 2 * hid), f32),
            pltpu.VMEM((listed * NZ, 2 * hid), f32),
            pltpu.VMEM((quarter, wide), f32),
            pltpu.VMEM((quarter, wide), f32),
            pltpu.VMEM((wide, wide), bf16),
            pltpu.VMEM((UNROLL * wide, 2 * GROUP * channels), bf16),
            pltpu.VMEM((quarter, GROUP * channels), f32),
            pltpu.VMEM((listed * NZ, UNROLL * wide), bf16),
            pltpu.VMEM((listed * NZ, 2 * GROUP * channels), f32),
            pltpu.VMEM((8, LANES), jnp.int32),
            pltpu.VMEM((count, 8, LANES), jnp.int32),
            pltpu.VMEM((blocks, cols_y, 2 * listed, lanes), f32),
            pltpu.VMEM((blocks, count, 2 * listed, lanes), f32),
            pltpu.VMEM((cols_y, blocks, quarter, LANES), f32),
            pltpu.VMEM((slots, blocks * 3 * depth), bf16),
            pltpu.VMEM((blocks * 3 * depth, lanes), bf16),
            pltpu.VMEM((slots, lanes), f32),
            pltpu.VMEM((slots, lanes), f32),
            pltpu.VMEM(parcel, f32),
            pltpu.VMEM(parcel, f32),
            pltpu.VMEM(last, f32),
            pltpu.SemaphoreType.DMA,
            pltpu.SemaphoreType.DMA((blocks + 4,)),
            pltpu.SemaphoreType.DMA((blocks + 4,)),
        ],
        compiler_params=pltpu.CompilerParams(collective_id=0, has_side_effects=True),
        name="encoder",
    )(
        tile_owner,
        tile_local,
        live_count,
        features,
        offsets,
        point_cell[None],
        w_first.T,
        b_first[None],
        w_second,
        b_second[None],
        w_third,
        z_table,
        backward,
        lift,
        w_modes,
    )


def decoder_kernel(
    codes_ref,
    held_ref,
    back_ref,
    inverse_ref,
    w_point_ref,
    b_point_ref,
    out_ref,
    rolled,
    before,
):
    cols_y, blocks, quarter = held_ref.shape[:3]
    channels = w_point_ref.shape[0]
    mine_y = lax.axis_index("gy")
    groups = LANES // channels
    lanes_w = back_ref.shape[2]
    own_q = lanes_w // channels
    value = back_ref[...].reshape(cols_y * 2 * CX * CY, lanes_w)
    if lanes_w < LANES:
        value = jnp.concatenate([value] * (LANES // lanes_w), 1)
    lane_tiles = value.shape[1] // LANES
    for lane_tile in range(lane_tiles):
        part = value[:, lane_tile * LANES : (lane_tile + 1) * LANES]
        for shift in range(groups):
            rolled[lane_tile, shift] = (
                pltpu.roll(part, shift * channels, 1) if shift else part
            )
    spans = 2 * cols_y
    lane = lax.broadcasted_iota(jnp.int32, (spans, LANES), 1) // channels
    bias = b_point_ref[...]
    for chunk in range(CX * CY // groups):
        rows = []
        for q in range(own_q):
            found = jnp.zeros((spans, LANES), f32)
            for j in range(groups):
                piece = rolled[
                    q // groups,
                    (j - q) % groups,
                    pl.ds(chunk * groups + j, spans, stride=CX * CY),
                    :,
                ]
                found = jnp.where(lane == j, piece, found)
            rows.append(found)
        table = jnp.concatenate(rows, 0)
        high, low = halves(table)
        spectral = lax.dot_general(
            jnp.concatenate([high, low, high], 0),
            inverse_ref[...],
            (((0,), (0,)), ((), ())),
            preferred_element_type=f32,
        )
        for j in range(groups):
            before[chunk * groups + j] = spectral[j * channels : (j + 1) * channels] + bias
    turned = w_point_ref[...].astype(f32).T.astype(bf16)
    turned = jnp.concatenate([turned, turned], 1)
    for source in range(cols_y):
        for block in range(blocks):
            tile = codes_ref[source, blocks + block, mine_y]

            @pl.when(tile >= 0)
            def _():
                flipped = held_ref[source, block].T
                item = jnp.concatenate(
                    [flipped[j * channels : (j + 1) * channels] for j in range(groups)], 1
                )
                high, low = halves(item)
                before[tile] += matmul(turned, jnp.concatenate([high, low], 0))

    root = math.sqrt(2.0 / math.pi)
    for tile in range(CX * CY):
        x = before[tile]
        half = 0.5 * x
        bent = jnp.tanh(x * (root + (0.044715 * root) * (x * x)))
        out_ref[tile // CY, tile % CY] = half + half * bent


def decoder(codes, held, back, inverse, w_point, b_point):
    smem = pl.BlockSpec(memory_space=pltpu.SMEM)
    vmem = pl.BlockSpec(memory_space=pltpu.VMEM)
    channels = w_point.shape[0]
    lane_tiles = max(1, back.shape[2] // LANES)
    rows = back.shape[0] * back.shape[1]
    return pl.pallas_call(
        decoder_kernel,
        out_shape=jax.ShapeDtypeStruct((CX, CY, channels, NZ), f32),
        in_specs=[smem] + [vmem] * 5,
        out_specs=vmem,
        scratch_shapes=[
            pltpu.VMEM((lane_tiles, LANES // channels, rows, LANES), f32),
            pltpu.VMEM((CX * CY, channels, NZ), f32),
        ],
        name="decoder",
    )(codes, held, back, inverse, w_point, b_point[:, None])


def local(
    features,
    offsets,
    point_cell,
    tile_owner,
    tile_local,
    live_count,
    w_first,
    b_first,
    w_second,
    b_second,
    w_third,
    w_point,
    b_point,
    w_modes,
):
    z_table, backward, lift, inverse = tables(
        lax.axis_size("gx"), lax.axis_size("gy"), w_modes.shape[0]
    )
    codes, held, back = encoder(
        features,
        offsets,
        point_cell,
        tile_owner,
        tile_local,
        live_count,
        w_first,
        b_first,
        w_second,
        b_second,
        w_third,
        w_modes,
        z_table,
        backward,
        lift,
    )
    return decoder(codes, held, back, inverse, w_point, b_point)


def solution(mesh):
    placed = (
        P(None, ("gx", "gy")),
        P(None, ("gx", "gy")),
        P(("gx", "gy")),
        P(("gx", "gy"), None),
        P(("gx", "gy"), None),
        P(("gx", "gy")),
        P(),
        P(),
        P(),
        P(),
        P(),
        P(),
        P(),
        P(None, "gx", "gy", None, None, None),
    )
    return jax.shard_map(
        local, mesh=mesh, in_specs=placed, out_specs=P("gx", "gy", None, None), check_vma=False
    )
```

```python
import math

import jax
import numpy as np
import jax.numpy as jnp
from jax import lax
from jax.experimental import pallas as pl
from jax.experimental.pallas import tpu as pltpu
from jax.sharding import PartitionSpec as P

NZ = 128
CX = 4
CY = 8
SPAN = 16
PB = 128
LANES = 128

GROUP = 4
UNROLL = 8

LINEAR = 2.0 * math.sqrt(2.0 / math.pi)
CUBIC = 4.0 * 0.044715 * LINEAR

f32 = jnp.float32
bf16 = jnp.bfloat16


def halves(value):
    high = value.astype(bf16)
    return high, (value - high.astype(f32)).astype(bf16)


def split_rows(value):
    high, low = halves(value)
    return jnp.concatenate([high, low, high], 0)


def split_table(table):
    table = np.asarray(table, np.float32)
    high = table.astype(jnp.bfloat16)
    low = (table - high.astype(np.float32)).astype(jnp.bfloat16)
    return np.concatenate([high, high, low], 1)


def matmul(left, right):
    return jnp.dot(left, right, preferred_element_type=f32)


def tables(cols_x, cols_y, modes):
    size_x, size_y = CX * cols_x, CY * cols_y
    own_p, own_q = modes // cols_x, modes // cols_y
    scale = 1.0 / math.sqrt(size_x * size_y * NZ)

    def frequencies(length):
        order = np.arange(modes)
        return np.where(order < modes // 2, order, length - modes + order)

    def turn(angle):
        cosine, sine = np.cos(angle), np.sin(angle)
        return np.array([[cosine, -sine], [sine, cosine]])

    z_turns = 2 * np.pi * (np.outer(np.arange(modes), np.arange(NZ)) % NZ) / NZ
    waves = np.stack([np.cos(z_turns), -np.sin(z_turns)], 0) * scale
    waves = waves.reshape(2, cols_y, own_q, NZ)
    z_table = waves.transpose(2, 0, 1, 3).reshape(-1, NZ)
    inverse = waves.transpose(2, 1, 0, 3).reshape(-1, NZ)
    inverse = np.asarray(inverse, np.float32)
    high = inverse.astype(jnp.bfloat16)
    low = (inverse - high.astype(np.float32)).astype(jnp.bfloat16)
    inverse = np.concatenate([high, high, low], 0)
    x_turns = 2 * np.pi * (np.outer(frequencies(size_x), np.arange(size_x)) % size_x) / size_x
    backward = turn(x_turns).reshape(2, 2, modes // 4, 4, cols_x, CX)
    backward = np.einsum("srgkdx,pP->dsPxpgrk", backward, np.eye(own_p))
    backward = backward.reshape(-1, modes * 2 * own_p)
    y_turns = 2 * np.pi * (np.outer(frequencies(size_y), np.arange(size_y)) % size_y) / size_y
    lift = turn(y_turns).reshape(2, 2, cols_x, own_p, cols_y, CY)
    lift = np.einsum("srepdy,xX->dsxyerpX", lift, np.eye(CX))
    lift = lift.reshape(2 * CX * size_y, -1)
    return split_table(z_table), split_table(backward), split_table(lift), inverse


def encoder_kernel(
    owner_ref,
    local_ref,
    live_ref,
    features_ref,
    offsets_ref,
    cells_ref,
    turned_first_ref,
    b_first_ref,
    w_second_ref,
    b_second_ref,
    w_third_ref,
    z_table_ref,
    backward_ref,
    lift_ref,
    modes_ref,
    codes_ref,
    held_ref,
    back_ref,
    weights,
    cell_sin,
    cell_cos,
    point_sin,
    point_cos,
    spread_two,
    spread_three,
    feats,
    second,
    sums,
    code_sent,
    code_got,
    sent_a,
    got_a,
    raw_sent,
    phases,
    splits,
    spectra,
    mixed,
    sent_d,
    got_d,
    sent_e,
    load_sem,
    sends,
    recvs,
):
    cols_x, cols_y = lax.axis_size("gx"), lax.axis_size("gy")
    mine_x, mine_y = lax.axis_index("gx"), lax.axis_index("gy")
    count = cols_x * cols_y
    me = mine_x * cols_y + mine_y
    blocks, listed = owner_ref.shape
    hid = w_second_ref.shape[0]
    channels = w_third_ref.shape[0]
    wide = GROUP * hid
    two = 2 * hid
    quarter = PB // GROUP
    size_x, size_y = CX * cols_x, CY * cols_y
    load = pltpu.make_async_copy(modes_ref, weights, load_sem)
    load.start()

    def everyone(body):
        if count <= 32:
            for step in range(1, count):
                body(step)
        else:
            pl.loop(1, count)(body)

    def place(step):
        other = lax.rem(me + step, count)
        return other // cols_y, lax.rem(other, cols_y)

    barrier = pltpu.get_barrier_semaphore()

    def greet(step):
        x, y = place(step)
        pl.semaphore_signal(barrier, inc=1, device_id={"gx": x, "gy": y})

    everyone(greet)

    turned_two = (w_second_ref[...].astype(f32).T * 0.5).astype(bf16)
    turned_three = w_third_ref[...].astype(f32).T
    spread_two[...] = jnp.zeros_like(spread_two)
    spread_three[...] = jnp.zeros_like(spread_three)
    for part in range(GROUP):
        rows = slice(part * hid, (part + 1) * hid)
        spread_two[rows, rows] = turned_two
    bias = jnp.concatenate([b_second_ref[...] * 0.5] * GROUP, 1)
    wide_three = jnp.concatenate([turned_three] * GROUP, 1)
    coarse_y, coarse_z = size_y // SPAN, NZ // SPAN
    cells = cells_ref[...]
    coarse = jnp.concatenate(
        [cells // (coarse_y * coarse_z), cells // coarse_z % coarse_y, cells % coarse_z], 0
    )
    places = coarse.astype(f32) * SPAN + offsets_ref[...].astype(f32)
    places = jnp.concatenate([places, jnp.zeros((5, places.shape[1]), f32)], 0)
    turned_first = turned_first_ref[...].astype(f32)
    double_first = jnp.concatenate([turned_first, turned_first], 1)
    features = features_ref[...].astype(f32)

    steps = lax.broadcasted_iota(jnp.int32, (24, two), 0)
    steps = jnp.where(steps < 16, steps * 8, steps - 16).astype(f32)
    steps = steps * double_first[2:3]
    cosine, sine = jnp.cos(steps), jnp.sin(steps)
    cos_fine, sin_fine = cosine[16:24], sine[16:24]
    bases = []
    for block in range(blocks):
        for slot in range(listed):
            tile = local_ref[block, slot]
            cell_x = (CX * mine_x + tile // CY).astype(f32)
            cell_y = (CY * owner_ref[block, slot] + tile % CY).astype(f32)
            bases.append(
                turned_first[0:1] * cell_x + turned_first[1:2] * cell_y + b_first_ref[...]
            )
    base = jnp.concatenate(bases, 0)
    base = jnp.concatenate([base, base], 1)
    base_sin, base_cos = jnp.sin(base), jnp.cos(base)
    code_lane = lax.broadcasted_iota(jnp.int32, (1, LANES), 1)
    code_rows = []
    for block in range(blocks):
        row = jnp.zeros((1, LANES), jnp.int32)
        for slot in range(listed):
            code = owner_ref[block, slot] * (CX * CY) + local_ref[block, slot]
            row = jnp.where(code_lane % listed == slot, code, row)
        code_rows.append(row)
    for block in range(blocks):
        row = jnp.full((1, LANES), -1, jnp.int32)
        for slot in range(listed):
            alive = jnp.where(slot < live_ref[block], local_ref[block, slot], -1)
            row = jnp.where(code_lane == owner_ref[block, slot], alive, row)
        code_rows.append(row)
    code_rows.append(jnp.zeros((8 - 2 * blocks, LANES), jnp.int32))
    code_sent[...] = jnp.concatenate(code_rows, 0)

    lane = lax.broadcasted_iota(jnp.int32, (quarter, two), 1)

    def pairs(block):
        here = slice(block * PB, (block + 1) * PB)
        for slot in range(listed):
            item = block * listed + slot
            b_sin, b_cos = base_sin[item : item + 1], base_cos[item : item + 1]
            near_sin = sin_fine * b_cos + cos_fine * b_sin
            near_cos = cos_fine * b_cos - sin_fine * b_sin
            for step in range(NZ // 8):
                rows = slice(slot * NZ + step * 8, slot * NZ + step * 8 + 8)
                far_cos, far_sin = cosine[step : step + 1], sine[step : step + 1]
                cell_sin[rows, :] = far_cos * near_sin + far_sin * near_cos
                cell_cos[rows, :] = far_cos * near_cos - far_sin * near_sin
        spots = places[:, here].T
        side = (
            double_first[0:1] * spots[:, 0:1]
            + double_first[1:2] * spots[:, 1:2]
            + double_first[2:3] * spots[:, 2:3]
        )
        side_cos, side_sin = jnp.cos(side), jnp.sin(side)
        for half in range(GROUP // 2):
            low = slice(2 * half * quarter, (2 * half + 1) * quarter)
            up = slice((2 * half + 1) * quarter, (2 * half + 2) * quarter)
            cols = slice(half * two, (half + 1) * two)
            point_cos[:, cols] = jnp.where(lane < hid, side_cos[low], side_cos[up])
            point_sin[:, cols] = jnp.where(lane < hid, side_sin[low], side_sin[up])
        turned = features[:, here].T
        feats[...] = jnp.concatenate(
            [turned[j * quarter : (j + 1) * quarter] for j in range(GROUP)], 1
        )
        sums[...] = jnp.zeros_like(sums)

        @pl.loop(0, quarter // UNROLL)
        def _(step):
            for inner in range(UNROLL):
                weigh = wide_three * feats[pl.ds(step * UNROLL + inner, 1), :]
                high, rest = halves(weigh)
                for part in range(GROUP):
                    rows = slice(inner * wide + part * hid, inner * wide + (part + 1) * hid)
                    cols = slice(part * channels, (part + 1) * channels)
                    spread_three[rows, part * channels : (part + 1) * channels] = high[:, cols]
                    spread_three[
                        rows, LANES + part * channels : LANES + (part + 1) * channels
                    ] = rest[:, cols]
            for slot in range(listed):
                rows = slice(slot * NZ, (slot + 1) * NZ)
                for inner in range(UNROLL):
                    group = step * UNROLL + inner
                    p_cos, p_sin = point_cos[pl.ds(group, 1), :], point_sin[pl.ds(group, 1), :]
                    c_sin, c_cos = cell_sin[rows, :], cell_cos[rows, :]
                    hidden = []
                    for half in range(GROUP // 2):
                        cols = slice(half * two, (half + 1) * two)
                        value = c_sin * p_cos[:, cols] - c_cos * p_sin[:, cols]
                        hidden.append(value.astype(bf16))
                    y = matmul(jnp.concatenate(hidden, 1), spread_two[...]) + bias
                    bent = jnp.tanh(y * (LINEAR + CUBIC * (y * y)))
                    second[rows, inner * wide : (inner + 1) * wide] = (y + y * bent).astype(bf16)
                sums[rows, :] += matmul(second[rows, :], spread_three[...])

    own_q = sent_a.shape[3] // channels
    lane_z = lax.broadcasted_iota(jnp.int32, (NZ, LANES), 1) // channels
    lane_r = lax.broadcasted_iota(jnp.int32, (quarter, LANES), 1) // channels
    scale = 1.0 / math.sqrt(PB)

    def parcels(block):
        flat = jnp.zeros((NZ, LANES), f32)
        dense = []
        for slot in range(listed):
            rows = slice(slot * NZ, (slot + 1) * NZ)
            total = sums[rows, 0:LANES] + sums[rows, LANES:]
            total = total + pltpu.roll(total, 2 * channels, 1)
            total = total + pltpu.roll(total, channels, 1)
            total = jnp.where(slot < live_ref[block], total * scale, 0.0)
            flat = jnp.where(lane_z == slot, total, flat)
            tight = total[0:quarter]
            for part in range(1, GROUP):
                tight = jnp.where(
                    lane_r == part, total[part * quarter : (part + 1) * quarter], tight
                )
            dense.append(tight)
        modes = matmul(z_table_ref[...], split_rows(flat))
        span = 2 * cols_y
        for slot in range(listed):
            lanes = slice(slot * channels, (slot + 1) * channels)
            joined = jnp.concatenate(
                [modes[q * span : (q + 1) * span, lanes] for q in range(own_q)], 1
            )
            for part in range(2):
                sent_a[block, :, part * listed + slot, :] = joined[
                    part * cols_y : (part + 1) * cols_y
                ]
        for dest in range(cols_y):
            chosen = jnp.zeros((quarter, LANES), f32)
            for slot in range(listed):
                chosen = jnp.where(owner_ref[block, slot] == dest, dense[slot], chosen)
            raw_sent[dest, block] = chosen

    def send(source, target, stage, x, y):
        pltpu.make_async_remote_copy(
            src_ref=source,
            dst_ref=target,
            send_sem=sends.at[stage],
            recv_sem=recvs.at[stage],
            device_id={"gx": x, "gy": y},
        ).start()

    def keep(source, target, stage):
        pltpu.make_async_copy(source, target, recvs.at[stage]).start()

    def spread(block):
        def go(step):
            x, y = place(step)
            send(sent_a.at[block, y], got_a.at[block, me], block, x, y)

        everyone(go)
        keep(sent_a.at[block, mine_y], got_a.at[block, me], block)

    def arrive(target, stage):
        pltpu.make_async_copy(target, target, recvs.at[stage]).wait()

    def depart(part, stage):
        pltpu.make_async_copy(part, part, sends.at[stage]).wait()

    stage_code, stage_raw, stage_d = blocks, blocks + 1, blocks + 2
    stage_e = stage_d + sent_d.shape[0]

    pairs(0)
    parcels(0)
    pl.semaphore_wait(barrier, count - 1)

    def tell(step):
        x, y = place(step)
        send(code_sent, code_got.at[me], stage_code, x, y)

    everyone(tell)
    keep(code_sent, code_got.at[me], stage_code)
    spread(0)
    for block in range(1, blocks):
        pairs(block)
        parcels(block)
        spread(block)

    for step in range(1, cols_y):
        other = lax.rem(mine_y + step, cols_y)
        send(raw_sent.at[other], held_ref.at[mine_y], stage_raw, mine_x, other)
    keep(raw_sent.at[mine_y], held_ref.at[mine_y], stage_raw)

    arrive(code_got, stage_code)
    own_p = sent_d.shape[2] // (2 * CX)
    modes = own_p * cols_x
    each = 2 * listed
    depth = count * each
    column = lax.broadcasted_iota(jnp.int32, (1, depth), 1)
    source = column // each
    slots = modes * 2
    row = lax.broadcasted_iota(jnp.int32, (slots, depth), 0)
    which = (row // 8) * 4 + row % 4
    freq_x = jnp.where(which < modes // 2, which, size_x - modes + which)
    part_out = (row // 4) % 2
    part_in = (column // listed) % 2
    quarters = (part_out - part_in).astype(f32) * 0.25
    p_at = mine_x * own_p + lax.broadcasted_iota(jnp.int32, (own_p, depth), 0)
    freq_y = jnp.where(p_at < modes // 2, p_at, size_y - modes + p_at)
    owns = (
        lax.broadcasted_iota(jnp.int32, (count, depth), 1) // each
        == lax.broadcasted_iota(jnp.int32, (count, depth), 0)
    )

    def waves(turns):
        angle = (turns - jnp.floor(turns)) * (2.0 * math.pi)
        return jnp.cos(angle), jnp.sin(angle)

    for block in range(blocks):
        codes = jnp.concatenate([code_got[:, block, :].astype(f32)] * (depth // LANES), 1)
        code = jnp.sum(jnp.where(owns, codes, 0.0), axis=0, keepdims=True).astype(jnp.int32)
        tile = code % (CX * CY)
        x_at = CX * (source // cols_y) + tile // CY
        y_at = CY * (code // (CX * CY)) + tile % CY
        x_cos, x_sin = waves((freq_x * x_at).astype(f32) * (1.0 / size_x) + quarters)
        y_cos, y_sin = waves((freq_y * y_at).astype(f32) * (1.0 / size_y))
        for p in range(own_p):
            value = x_cos * y_cos[p : p + 1] - x_sin * y_sin[p : p + 1]
            high, low = halves(value)
            rows = slice(p * slots, (p + 1) * slots)
            start = block * 3 * depth
            phases[rows, start : start + depth] = high
            phases[rows, start + depth : start + 2 * depth] = high
            phases[rows, start + 2 * depth : start + 3 * depth] = low
    lanes_w = got_a.shape[3]
    for block in range(blocks):
        arrive(got_a.at[block], block)
        splits[block * 3 * depth : (block + 1) * 3 * depth, :] = split_rows(
            got_a[block].reshape(depth, lanes_w)
        )
    spectra[...] = matmul(phases[...], splits[...])

    load.wait()
    pieces, width = sent_d.shape[0], sent_d.shape[3]
    quad = 8 * channels
    bands = LANES // channels
    row_of = lax.broadcasted_iota(jnp.int32, (8, LANES), 0)
    lane_of = lax.broadcasted_iota(jnp.int32, (8, LANES), 1)
    band = lane_of // channels
    own_four = [row_of % 4 == 2 * side + lane_of // (2 * channels) for side in range(2)]
    negate = row_of < 4
    fours = modes // 4
    ahead = 8

    for piece in range(pieces):
        first_q = piece * (width // channels)

        @pl.loop(0, own_p * fours // ahead)
        def _(outer):
            for inner in range(ahead):
                group = outer * ahead + inner
                p = group // fours
                low = (group % fours) * 4
                start = pl.multiple_of(group * 8, 8)
                plain = spectra[pl.ds(start, 8), piece * width : (piece + 1) * width]
                plain = jnp.concatenate([plain] * (LANES // width), 1)
                turned = pltpu.roll(plain, 4, 0)
                turned = jnp.where(negate, -turned, turned)
                plains = [plain] + [pltpu.roll(plain, r * channels, 1) for r in range(1, bands)]
                turns = [turned] + [pltpu.roll(turned, r * channels, 1) for r in range(1, bands)]
                outs = []
                for q in range(width // channels):
                    both = plains[-q % bands]
                    for at in range(1, bands):
                        kind = turns if at % 2 else plains
                        both = jnp.where(band == at, kind[(at - q) % bands], both)
                    both = jnp.concatenate([jnp.where(own, both, 0.0) for own in own_four], 1)
                    high, rest = halves(both)
                    tile = weights[pl.ds(low, 4), p, first_q + q].reshape(quad, channels)
                    out = matmul(jnp.concatenate([high, rest], 0), tile)
                    outs.append(out[:8] + out[8:])
                mixed[pl.ds(start, 8), piece * width : (piece + 1) * width] = jnp.concatenate(
                    outs, 1
                )

        along_x = matmul(
            backward_ref[...], split_rows(mixed[:, piece * width : (piece + 1) * width])
        )
        sent_d[piece] = along_x.reshape(sent_d.shape[1:])
        for step in range(1, cols_x):
            other = lax.rem(mine_x + step, cols_x)
            send(
                sent_d.at[piece, other],
                got_d.at[piece, mine_x],
                stage_d + piece,
                other,
                mine_y,
            )
        keep(sent_d.at[piece, mine_x], got_d.at[piece, mine_x], stage_d + piece)
    for piece in range(pieces):
        arrive(got_d.at[piece], stage_d + piece)
        along_y = matmul(lift_ref[...], split_rows(got_d[piece].reshape(-1, width)))
        sent_e[piece] = along_y.reshape(sent_e.shape[1:])
        for step in range(1, cols_y):
            other = lax.rem(mine_y + step, cols_y)
            send(
                sent_e.at[piece, other],
                back_ref.at[piece, mine_y],
                stage_e + piece,
                mine_x,
                other,
            )
        keep(sent_e.at[piece, mine_y], back_ref.at[piece, mine_y], stage_e + piece)
    codes_ref[...] = code_got[pl.ds(mine_x * cols_y, cols_y)]
    for block in range(blocks):
        depart(got_a.at[block, pl.ds(0, count - 1)], block)
    depart(code_got.at[pl.ds(0, count - 1)], stage_code)
    depart(raw_sent.at[pl.ds(0, cols_y - 1)], stage_raw)
    for piece in range(pieces):
        depart(sent_d.at[piece, pl.ds(0, cols_x - 1)], stage_d + piece)
    arrive(held_ref, stage_raw)
    for piece in range(pieces):
        arrive(back_ref.at[piece], stage_e + piece)
        depart(sent_e.at[piece, pl.ds(0, cols_y - 1)], stage_e + piece)


def encoder(
    features,
    offsets,
    point_cell,
    tile_owner,
    tile_local,
    live_count,
    w_first,
    b_first,
    w_second,
    b_second,
    w_third,
    w_modes,
    z_table,
    backward,
    lift,
):
    cols_x, cols_y = lax.axis_size("gx"), lax.axis_size("gy")
    count = cols_x * cols_y
    own_p, own_q = w_modes.shape[1:3]
    modes, channels = w_modes.shape[0], w_modes.shape[-1]
    hid = w_third.shape[1]
    blocks, listed = tile_owner.shape
    lanes = own_q * channels
    wide = GROUP * hid
    quarter = PB // GROUP
    depth = count * 2 * listed
    slots = modes * 2 * own_p
    smem = pl.BlockSpec(memory_space=pltpu.SMEM)
    vmem = pl.BlockSpec(memory_space=pltpu.VMEM)
    pieces = max(1, lanes // LANES)
    width = lanes // pieces
    last = (pieces, cols_y, 2 * CX * CY, width)
    parcel = (pieces, cols_x, 2 * own_p * CX, width)
    stages = blocks + 2 + 2 * pieces
    return pl.pallas_call(
        encoder_kernel,
        out_shape=(
            jax.ShapeDtypeStruct((cols_y, 8, LANES), jnp.int32),
            jax.ShapeDtypeStruct((cols_y, blocks, quarter, LANES), f32),
            jax.ShapeDtypeStruct(last, f32),
        ),
        in_specs=[smem] * 3 + [vmem] * 11 + [pl.BlockSpec(memory_space=pl.ANY)],
        out_specs=(vmem, vmem, vmem),
        scratch_shapes=[
            pltpu.VMEM(w_modes.shape, w_modes.dtype),
            pltpu.VMEM((listed * NZ, 2 * hid), f32),
            pltpu.VMEM((listed * NZ, 2 * hid), f32),
            pltpu.VMEM((quarter, wide), f32),
            pltpu.VMEM((quarter, wide), f32),
            pltpu.VMEM((wide, wide), bf16),
            pltpu.VMEM((UNROLL * wide, 2 * GROUP * channels), bf16),
            pltpu.VMEM((quarter, GROUP * channels), f32),
            pltpu.VMEM((listed * NZ, UNROLL * wide), bf16),
            pltpu.VMEM((listed * NZ, 2 * GROUP * channels), f32),
            pltpu.VMEM((8, LANES), jnp.int32),
            pltpu.VMEM((count, 8, LANES), jnp.int32),
            pltpu.VMEM((blocks, cols_y, 2 * listed, lanes), f32),
            pltpu.VMEM((blocks, count, 2 * listed, lanes), f32),
            pltpu.VMEM((cols_y, blocks, quarter, LANES), f32),
            pltpu.VMEM((slots, blocks * 3 * depth), bf16),
            pltpu.VMEM((blocks * 3 * depth, lanes), bf16),
            pltpu.VMEM((slots, lanes), f32),
            pltpu.VMEM((slots, lanes), f32),
            pltpu.VMEM(parcel, f32),
            pltpu.VMEM(parcel, f32),
            pltpu.VMEM(last, f32),
            pltpu.SemaphoreType.DMA,
            pltpu.SemaphoreType.DMA((stages,)),
            pltpu.SemaphoreType.DMA((stages,)),
        ],
        compiler_params=pltpu.CompilerParams(collective_id=0, has_side_effects=True),
        name="encoder",
    )(
        tile_owner,
        tile_local,
        live_count,
        features,
        offsets,
        point_cell[None],
        w_first.T,
        b_first[None],
        w_second,
        b_second[None],
        w_third,
        z_table,
        backward,
        lift,
        w_modes,
    )


def decoder_kernel(
    codes_ref,
    held_ref,
    back_ref,
    inverse_ref,
    w_point_ref,
    b_point_ref,
    out_ref,
    rolled,
    before,
    done,
    out_sem,
):
    cols_y, blocks, quarter = held_ref.shape[:3]
    channels = w_point_ref.shape[0]
    mine_y = lax.axis_index("gy")
    groups = LANES // channels
    pieces, width = back_ref.shape[0], back_ref.shape[3]
    each = width // channels
    bias = jnp.concatenate([b_point_ref[...]] * channels, 0).T[:, 0:1]
    before[...] = jnp.zeros_like(before)
    turned = w_point_ref[...].astype(f32).T.astype(bf16)
    turned = jnp.concatenate([turned, turned], 1)
    items = []
    for source in range(cols_y):
        for block in range(blocks):
            flipped = held_ref[source, block].T
            items.append(
                jnp.concatenate(
                    [flipped[j * channels : (j + 1) * channels] for j in range(groups)], 1
                )
            )
    high, low = halves(jnp.concatenate(items, 1))
    points = matmul(turned, jnp.concatenate([high, low], 0))
    for source in range(cols_y):
        for block in range(blocks):
            tile = codes_ref[source, blocks + block, mine_y]
            item = source * blocks + block

            @pl.when(tile >= 0)
            def _():
                before[tile] += points[:, item * NZ : (item + 1) * NZ]

    for piece in range(pieces):
        value = back_ref[piece].reshape(cols_y * 2 * CX * CY, width)
        value = jnp.concatenate([value] * (LANES // width), 1)
        for shift in range(groups):
            rolled[piece, shift] = pltpu.roll(value, shift * channels, 1) if shift else value
    spans = 2 * cols_y
    lane = lax.broadcasted_iota(jnp.int32, (spans, LANES), 1) // channels
    root = math.sqrt(2.0 / math.pi)
    moves = []
    for chunk in range(CX * CY // groups):
        rows = []
        for q in range(pieces * each):
            found = jnp.zeros((spans, LANES), f32)
            for j in range(groups):
                piece = rolled[
                    q // each,
                    (j - q % each) % groups,
                    pl.ds(chunk * groups + j, spans, stride=CX * CY),
                    :,
                ]
                found = jnp.where(lane == j, piece, found)
            rows.append(found)
        spectral = lax.dot_general(
            split_rows(jnp.concatenate(rows, 0)),
            inverse_ref[...],
            (((0,), (0,)), ((), ())),
            preferred_element_type=f32,
        )
        for j in range(groups):
            tile = chunk * groups + j
            x = spectral[j * channels : (j + 1) * channels] + (before[tile] + bias)
            half = 0.5 * x
            bent = jnp.tanh(x * (root + (0.044715 * root) * (x * x)))
            done[tile // CY, tile % CY] = half + half * bent
        at = (chunk * groups // CY, pl.ds(chunk * groups % CY, groups))
        move = pltpu.make_async_copy(done.at[at], out_ref.at[at], out_sem.at[chunk])
        move.start()
        moves.append(move)
    for move in moves:
        move.wait()


def decoder(codes, held, back, inverse, w_point, b_point):
    smem = pl.BlockSpec(memory_space=pltpu.SMEM)
    vmem = pl.BlockSpec(memory_space=pltpu.VMEM)
    channels = w_point.shape[0]
    rows = back.shape[1] * back.shape[2]
    shape = (CX, CY, channels, NZ)
    return pl.pallas_call(
        decoder_kernel,
        out_shape=jax.ShapeDtypeStruct(shape, f32),
        in_specs=[smem] + [vmem] * 5,
        out_specs=pl.BlockSpec(memory_space=pl.ANY),
        scratch_shapes=[
            pltpu.VMEM((back.shape[0], LANES // channels, rows, LANES), f32),
            pltpu.VMEM((CX * CY, channels, NZ), f32),
            pltpu.VMEM(shape, f32),
            pltpu.SemaphoreType.DMA((CX * CY * channels // LANES,)),
        ],
        name="decoder",
    )(codes, held, back, inverse, w_point, b_point[None])


def local(
    features,
    offsets,
    point_cell,
    tile_owner,
    tile_local,
    live_count,
    w_first,
    b_first,
    w_second,
    b_second,
    w_third,
    w_point,
    b_point,
    w_modes,
):
    z_table, backward, lift, inverse = tables(
        lax.axis_size("gx"), lax.axis_size("gy"), w_modes.shape[0]
    )
    codes, held, back = encoder(
        features,
        offsets,
        point_cell,
        tile_owner,
        tile_local,
        live_count,
        w_first,
        b_first,
        w_second,
        b_second,
        w_third,
        w_modes,
        z_table,
        backward,
        lift,
    )
    return decoder(codes, held, back, inverse, w_point, b_point)


def solution(mesh):
    placed = (
        P(None, ("gx", "gy")),
        P(None, ("gx", "gy")),
        P(("gx", "gy")),
        P(("gx", "gy"), None),
        P(("gx", "gy"), None),
        P(("gx", "gy")),
        P(),
        P(),
        P(),
        P(),
        P(),
        P(),
        P(),
        P(None, "gx", "gy", None, None, None),
    )
    return jax.shard_map(
        local, mesh=mesh, in_specs=placed, out_specs=P("gx", "gy", None, None), check_vma=False
    )
```

```python
import math

import jax
import numpy as np
import jax.numpy as jnp
from jax import lax
from jax.experimental import pallas as pl
from jax.experimental.pallas import tpu as pltpu
from jax.sharding import PartitionSpec as P

NZ = 128
CX = 4
CY = 8
SPAN = 16
PB = 128
LANES = 128

GROUP = 4
UNROLL = 16

LINEAR = 2.0 * math.sqrt(2.0 / math.pi)
CUBIC = 4.0 * 0.044715 * LINEAR

f32 = jnp.float32
bf16 = jnp.bfloat16


def halves(value):
    high = value.astype(bf16)
    return high, (value - high.astype(f32)).astype(bf16)


def split_rows(value):
    high, low = halves(value)
    return jnp.concatenate([high, low, high], 0)


def split_table(table):
    table = np.asarray(table, np.float32)
    high = table.astype(jnp.bfloat16)
    low = (table - high.astype(np.float32)).astype(jnp.bfloat16)
    return np.concatenate([high, high, low], 1)


def matmul(left, right):
    return jnp.dot(left, right, preferred_element_type=f32)


def tables(cols_x, cols_y, modes):
    size_x, size_y = CX * cols_x, CY * cols_y
    own_p, own_q = modes // cols_x, modes // cols_y
    scale = 1.0 / math.sqrt(size_x * size_y * NZ)

    def frequencies(length):
        order = np.arange(modes)
        return np.where(order < modes // 2, order, length - modes + order)

    def turn(angle):
        cosine, sine = np.cos(angle), np.sin(angle)
        return np.array([[cosine, -sine], [sine, cosine]])

    z_turns = 2 * np.pi * (np.outer(np.arange(modes), np.arange(NZ)) % NZ) / NZ
    waves = np.stack([np.cos(z_turns), -np.sin(z_turns)], 0) * scale
    waves = waves.reshape(2, cols_y, own_q, NZ)
    z_table = waves.transpose(2, 0, 1, 3).reshape(-1, NZ)
    inverse = waves.transpose(2, 1, 0, 3).reshape(-1, NZ)
    inverse = np.asarray(inverse, np.float32)
    high = inverse.astype(jnp.bfloat16)
    low = (inverse - high.astype(np.float32)).astype(jnp.bfloat16)
    inverse = np.concatenate([high, high, low], 0)
    x_turns = 2 * np.pi * (np.outer(frequencies(size_x), np.arange(size_x)) % size_x) / size_x
    backward = turn(x_turns).reshape(2, 2, modes // 4, 4, cols_x, CX)
    backward = np.einsum("srgkdx,pP->dsPxpgrk", backward, np.eye(own_p))
    backward = backward.reshape(-1, modes * 2 * own_p)
    y_turns = 2 * np.pi * (np.outer(frequencies(size_y), np.arange(size_y)) % size_y) / size_y
    lift = turn(y_turns).reshape(2, 2, cols_x, own_p, cols_y, CY)
    lift = np.einsum("srepdy,xX->dsxyerpX", lift, np.eye(CX))
    lift = lift.reshape(2 * CX * size_y, -1)
    return split_table(z_table), split_table(backward), split_table(lift), inverse


def parts_of(blocks, listed):
    whole = [(block, 0, listed) for block in range(blocks - 1)]
    half = listed // 2
    return whole + [(blocks - 1, 0, half), (blocks - 1, half, listed - half)]


def encoder_kernel(
    owner_ref,
    local_ref,
    live_ref,
    features_ref,
    offsets_ref,
    cells_ref,
    turned_first_ref,
    b_first_ref,
    w_second_ref,
    b_second_ref,
    w_third_ref,
    z_table_ref,
    backward_hbm,
    lift_hbm,
    modes_ref,
    codes_ref,
    held_ref,
    back_ref,
    weights,
    backward_ref,
    lift_ref,
    cell_sin,
    cell_cos,
    point_sin,
    point_cos,
    spread_two,
    spread_three,
    feats,
    second,
    sums,
    dense,
    code_sent,
    code_got,
    sent_a,
    got_a,
    raw_sent,
    phases,
    splits,
    spectra,
    mixed,
    sent_d,
    got_d,
    sent_e,
    load_sem,
    sends,
    recvs,
):
    cols_x, cols_y = lax.axis_size("gx"), lax.axis_size("gy")
    mine_x, mine_y = lax.axis_index("gx"), lax.axis_index("gy")
    count = cols_x * cols_y
    me = mine_x * cols_y + mine_y
    blocks, listed = owner_ref.shape
    hid = w_second_ref.shape[0]
    channels = w_third_ref.shape[0]
    wide = GROUP * hid
    two = 2 * hid
    quarter = PB // GROUP
    size_x, size_y = CX * cols_x, CY * cols_y
    loads = []
    for index, (source, target) in enumerate(
        ((modes_ref, weights), (backward_hbm, backward_ref), (lift_hbm, lift_ref))
    ):
        load = pltpu.make_async_copy(source, target, load_sem.at[index])
        load.start()
        loads.append(load)

    def everyone(body):
        if count <= 32:
            for step in range(1, count):
                body(step)
        else:
            pl.loop(1, count)(body)

    def place(step):
        other = lax.rem(me + step, count)
        return other // cols_y, lax.rem(other, cols_y)

    barrier = pltpu.get_barrier_semaphore()

    def greet(step):
        x, y = place(step)
        pl.semaphore_signal(barrier, inc=1, device_id={"gx": x, "gy": y})

    everyone(greet)

    turned_two = (w_second_ref[...].astype(f32).T * 0.5).astype(bf16)
    turned_three = w_third_ref[...].astype(f32).T
    spread_two[...] = jnp.zeros_like(spread_two)
    spread_three[...] = jnp.zeros_like(spread_three)
    for part in range(GROUP):
        rows = slice(part * hid, (part + 1) * hid)
        spread_two[rows, rows] = turned_two
    bias = jnp.concatenate([b_second_ref[...] * 0.5] * GROUP, 1)
    wide_three = jnp.concatenate([turned_three] * GROUP, 1)
    coarse_y, coarse_z = size_y // SPAN, NZ // SPAN
    cells = cells_ref[...]
    coarse = jnp.concatenate(
        [cells // (coarse_y * coarse_z), cells // coarse_z % coarse_y, cells % coarse_z], 0
    )
    places = coarse.astype(f32) * SPAN + offsets_ref[...].astype(f32)
    places = jnp.concatenate([places, jnp.zeros((5, places.shape[1]), f32)], 0)
    turned_first = turned_first_ref[...].astype(f32)
    double_first = jnp.concatenate([turned_first, turned_first], 1)
    features = features_ref[...].astype(f32)

    steps = lax.broadcasted_iota(jnp.int32, (24, two), 0)
    steps = jnp.where(steps < 16, steps * 8, steps - 16).astype(f32)
    steps = steps * double_first[2:3]
    cosine, sine = jnp.cos(steps), jnp.sin(steps)
    cos_fine, sin_fine = cosine[16:24], sine[16:24]
    bases = []
    for block in range(blocks):
        for slot in range(listed):
            tile = local_ref[block, slot]
            cell_x = (CX * mine_x + tile // CY).astype(f32)
            cell_y = (CY * owner_ref[block, slot] + tile % CY).astype(f32)
            bases.append(
                turned_first[0:1] * cell_x + turned_first[1:2] * cell_y + b_first_ref[...]
            )
    base = jnp.concatenate(bases, 0)
    base = jnp.concatenate([base, base], 1)
    base_sin, base_cos = jnp.sin(base), jnp.cos(base)
    code_lane = lax.broadcasted_iota(jnp.int32, (1, LANES), 1)
    code_rows = []
    parts = parts_of(blocks, listed)
    for block, begin, some in parts:
        row = jnp.zeros((1, LANES), jnp.int32)
        for slot in range(some):
            code = (
                owner_ref[block, begin + slot] * (CX * CY) + local_ref[block, begin + slot]
            )
            row = jnp.where(code_lane % some == slot, code, row)
        code_rows.append(row)
    for block in range(blocks):
        row = jnp.full((1, LANES), -1, jnp.int32)
        for slot in range(listed):
            alive = jnp.where(slot < live_ref[block], local_ref[block, slot], -1)
            row = jnp.where(code_lane == owner_ref[block, slot], alive, row)
        code_rows.append(row)
    code_rows.append(jnp.zeros((8 - len(code_rows), LANES), jnp.int32))
    code_sent[...] = jnp.concatenate(code_rows, 0)

    lane = lax.broadcasted_iota(jnp.int32, (quarter, two), 1)

    def points(block):
        here = slice(block * PB, (block + 1) * PB)
        spots = places[:, here].T
        for half in range(GROUP // 2):
            low = slice(2 * half * quarter, (2 * half + 1) * quarter)
            up = slice((2 * half + 1) * quarter, (2 * half + 2) * quarter)
            cols = slice(half * two, (half + 1) * two)
            side = 0.0
            for axis in range(3):
                spot = jnp.where(lane < hid, spots[low, axis : axis + 1], spots[up, axis : axis + 1])
                side = side + double_first[axis : axis + 1] * spot
            point_cos[:, cols] = jnp.cos(side)
            point_sin[:, cols] = jnp.sin(side)
        turned = features[:, here].T
        feats[...] = jnp.concatenate(
            [turned[j * quarter : (j + 1) * quarter] for j in range(GROUP)], 1
        )

    def pairs(block, begin, some):
        for slot in range(some):
            item = block * listed + begin + slot
            b_sin, b_cos = base_sin[item : item + 1], base_cos[item : item + 1]
            near_sin = sin_fine * b_cos + cos_fine * b_sin
            near_cos = cos_fine * b_cos - sin_fine * b_sin
            for step in range(NZ // 8):
                rows = slice(slot * NZ + step * 8, slot * NZ + step * 8 + 8)
                far_cos, far_sin = cosine[step : step + 1], sine[step : step + 1]
                cell_sin[rows, :] = far_cos * near_sin + far_sin * near_cos
                cell_cos[rows, :] = far_cos * near_cos - far_sin * near_sin
        sums[...] = jnp.zeros_like(sums)

        @pl.loop(0, quarter // UNROLL)
        def _(step):
            for inner in range(UNROLL):
                weigh = wide_three * feats[pl.ds(step * UNROLL + inner, 1), :]
                high, rest = halves(weigh)
                for part in range(GROUP):
                    rows = slice(inner * wide + part * hid, inner * wide + (part + 1) * hid)
                    cols = slice(part * channels, (part + 1) * channels)
                    spread_three[rows, part * channels : (part + 1) * channels] = high[:, cols]
                    spread_three[
                        rows, LANES + part * channels : LANES + (part + 1) * channels
                    ] = rest[:, cols]
            for slot in range(some):
                rows = slice(slot * NZ, (slot + 1) * NZ)
                for inner in range(UNROLL):
                    group = step * UNROLL + inner
                    p_cos, p_sin = point_cos[pl.ds(group, 1), :], point_sin[pl.ds(group, 1), :]
                    c_sin, c_cos = cell_sin[rows, :], cell_cos[rows, :]
                    hidden = []
                    for half in range(GROUP // 2):
                        cols = slice(half * two, (half + 1) * two)
                        value = c_sin * p_cos[:, cols] - c_cos * p_sin[:, cols]
                        hidden.append(value.astype(bf16))
                    y = matmul(jnp.concatenate(hidden, 1), spread_two[...]) + bias
                    bent = jnp.tanh(y * (LINEAR + CUBIC * (y * y)))
                    second[rows, inner * wide : (inner + 1) * wide] = (y + y * bent).astype(bf16)
                sums[rows, :] += matmul(second[rows, :], spread_three[...])

    own_q = sent_a.shape[3] // channels
    lane_z = lax.broadcasted_iota(jnp.int32, (NZ, LANES), 1) // channels
    lane_r = lax.broadcasted_iota(jnp.int32, (quarter, LANES), 1) // channels
    scale = 1.0 / math.sqrt(PB)

    def parcels(part):
        block, begin, some = parts[part]
        flat = jnp.zeros((NZ, LANES), f32)
        for slot in range(some):
            rows = slice(slot * NZ, (slot + 1) * NZ)
            total = sums[rows, 0:LANES] + sums[rows, LANES:]
            total = total + pltpu.roll(total, 2 * channels, 1)
            total = total + pltpu.roll(total, channels, 1)
            total = jnp.where(begin + slot < live_ref[block], total * scale, 0.0)
            flat = jnp.where(lane_z == slot, total, flat)
            tight = total[0:quarter]
            for at in range(1, GROUP):
                tight = jnp.where(lane_r == at, total[at * quarter : (at + 1) * quarter], tight)
            dense[begin + slot] = tight
        modes = matmul(z_table_ref[...], split_rows(flat))
        span = 2 * cols_y
        for slot in range(some):
            lanes = slice(slot * channels, (slot + 1) * channels)
            joined = jnp.concatenate(
                [modes[q * span : (q + 1) * span, lanes] for q in range(own_q)], 1
            )
            for half in range(2):
                sent_a[part, :, half * some + slot, :] = joined[
                    half * cols_y : (half + 1) * cols_y
                ]

    def raws(block):
        for dest in range(cols_y):
            chosen = jnp.zeros((quarter, LANES), f32)
            for slot in range(listed):
                chosen = jnp.where(owner_ref[block, slot] == dest, dense[slot], chosen)
            raw_sent[dest, block] = chosen

    def send(source, target, stage, x, y):
        pltpu.make_async_remote_copy(
            src_ref=source,
            dst_ref=target,
            send_sem=sends.at[stage],
            recv_sem=recvs.at[stage],
            device_id={"gx": x, "gy": y},
        ).start()

    def keep(source, target, stage):
        pltpu.make_async_copy(source, target, recvs.at[stage]).start()

    def spread(part):
        rows = pl.ds(0, 2 * parts[part][2])

        def go(step):
            x, y = place(step)
            send(sent_a.at[part, y, rows], got_a.at[part, me, rows], part, x, y)

        everyone(go)
        keep(sent_a.at[part, mine_y, rows], got_a.at[part, me, rows], part)

    def arrive(target, stage):
        pltpu.make_async_copy(target, target, recvs.at[stage]).wait()

    def depart(part, stage):
        pltpu.make_async_copy(part, part, sends.at[stage]).wait()

    stage_code = len(parts)
    stage_raw, stage_d = stage_code + 1, stage_code + 2
    stage_e = stage_d + sent_d.shape[0]

    for part, (block, begin, some) in enumerate(parts):
        if begin == 0:
            points(block)
        pairs(block, begin, some)
        parcels(part)
        if part == 0:
            pl.semaphore_wait(barrier, count - 1)

            def tell(step):
                x, y = place(step)
                send(code_sent, code_got.at[me], stage_code, x, y)

            everyone(tell)
            keep(code_sent, code_got.at[me], stage_code)
        spread(part)
        if begin + some == listed:
            raws(block)

    for step in range(1, cols_y):
        other = lax.rem(mine_y + step, cols_y)
        send(raw_sent.at[other], held_ref.at[mine_y], stage_raw, mine_x, other)
    keep(raw_sent.at[mine_y], held_ref.at[mine_y], stage_raw)

    arrive(code_got, stage_code)
    own_p = sent_d.shape[2] // (2 * CX)
    modes = own_p * cols_x
    slots = modes * 2
    lanes_w = got_a.shape[3]

    def waves(turns):
        angle = (turns - jnp.floor(turns)) * (2.0 * math.pi)
        return jnp.cos(angle), jnp.sin(angle)

    starts = [0]
    for part, (block, begin, some) in enumerate(parts):
        each = 2 * some
        depth = count * each
        column = lax.broadcasted_iota(jnp.int32, (1, depth), 1)
        source = column // each
        row = lax.broadcasted_iota(jnp.int32, (slots, depth), 0)
        which = (row // 8) * 4 + row % 4
        freq_x = jnp.where(which < modes // 2, which, size_x - modes + which)
        part_out = (row // 4) % 2
        part_in = (column // some) % 2
        quarters = (part_out - part_in).astype(f32) * 0.25
        p_at = mine_x * own_p + lax.broadcasted_iota(jnp.int32, (own_p, depth), 0)
        freq_y = jnp.where(p_at < modes // 2, p_at, size_y - modes + p_at)
        owns = (
            lax.broadcasted_iota(jnp.int32, (count, depth), 1) // each
            == lax.broadcasted_iota(jnp.int32, (count, depth), 0)
        )
        codes = jnp.concatenate([code_got[:, part, :].astype(f32)] * (depth // LANES), 1)
        code = jnp.sum(jnp.where(owns, codes, 0.0), axis=0, keepdims=True).astype(jnp.int32)
        tile = code % (CX * CY)
        x_at = CX * (source // cols_y) + tile // CY
        y_at = CY * (code // (CX * CY)) + tile % CY
        x_cos, x_sin = waves((freq_x * x_at).astype(f32) * (1.0 / size_x) + quarters)
        y_cos, y_sin = waves((freq_y * y_at).astype(f32) * (1.0 / size_y))
        start = starts[part]
        for p in range(own_p):
            value = x_cos * y_cos[p : p + 1] - x_sin * y_sin[p : p + 1]
            high, low = halves(value)
            rows = slice(p * slots, (p + 1) * slots)
            phases[rows, start : start + depth] = high
            phases[rows, start + depth : start + 2 * depth] = high
            phases[rows, start + 2 * depth : start + 3 * depth] = low
        starts.append(start + 3 * depth)
    for part, (block, begin, some) in enumerate(parts):
        rows = pl.ds(0, 2 * some)
        arrive(got_a.at[part, :, rows], part)
        splits[starts[part] : starts[part + 1], :] = split_rows(
            got_a[part, :, 0 : 2 * some].reshape(count * 2 * some, lanes_w)
        )
        if part == len(parts) - 2:
            seen = slice(0, starts[part + 1])
            spectra[...] = matmul(phases[:, seen], splits[seen, :])
    seen = slice(starts[-2], starts[-1])
    spectra[...] += matmul(phases[:, seen], splits[seen, :])

    for load in loads:
        load.wait()
    pieces, width = sent_d.shape[0], sent_d.shape[3]
    quad = 8 * channels
    bands = LANES // channels
    row_of = lax.broadcasted_iota(jnp.int32, (8, LANES), 0)
    lane_of = lax.broadcasted_iota(jnp.int32, (8, LANES), 1)
    band = lane_of // channels
    own_four = [row_of % 4 == 2 * side + lane_of // (2 * channels) for side in range(2)]
    negate = row_of < 4
    fours = modes // 4
    ahead = 8

    for piece in range(pieces):
        first_q = piece * (width // channels)

        @pl.loop(0, own_p * fours // ahead)
        def _(outer):
            for inner in range(ahead):
                group = outer * ahead + inner
                p = group // fours
                low = (group % fours) * 4
                start = pl.multiple_of(group * 8, 8)
                plain = spectra[pl.ds(start, 8), piece * width : (piece + 1) * width]
                plain = jnp.concatenate([plain] * (LANES // width), 1)
                turned = pltpu.roll(plain, 4, 0)
                turned = jnp.where(negate, -turned, turned)
                plains = [plain] + [pltpu.roll(plain, r * channels, 1) for r in range(1, bands)]
                turns = [turned] + [pltpu.roll(turned, r * channels, 1) for r in range(1, bands)]
                outs = []
                for q in range(width // channels):
                    both = plains[-q % bands]
                    for at in range(1, bands):
                        kind = turns if at % 2 else plains
                        both = jnp.where(band == at, kind[(at - q) % bands], both)
                    both = jnp.concatenate([jnp.where(own, both, 0.0) for own in own_four], 1)
                    high, rest = halves(both)
                    tile = weights[pl.ds(low, 4), p, first_q + q].reshape(quad, channels)
                    out = matmul(jnp.concatenate([high, rest], 0), tile)
                    outs.append(out[:8] + out[8:])
                mixed[pl.ds(start, 8), piece * width : (piece + 1) * width] = jnp.concatenate(
                    outs, 1
                )

        along_x = matmul(
            backward_ref[...], split_rows(mixed[:, piece * width : (piece + 1) * width])
        )
        sent_d[piece] = along_x.reshape(sent_d.shape[1:])
        for step in range(1, cols_x):
            other = lax.rem(mine_x + step, cols_x)
            send(
                sent_d.at[piece, other],
                got_d.at[piece, mine_x],
                stage_d + piece,
                other,
                mine_y,
            )
        keep(sent_d.at[piece, mine_x], got_d.at[piece, mine_x], stage_d + piece)
    for piece in range(pieces):
        arrive(got_d.at[piece], stage_d + piece)
        along_y = matmul(lift_ref[...], split_rows(got_d[piece].reshape(-1, width)))
        sent_e[piece] = along_y.reshape(sent_e.shape[1:])
        for step in range(1, cols_y):
            other = lax.rem(mine_y + step, cols_y)
            send(
                sent_e.at[piece, other],
                back_ref.at[piece, mine_y],
                stage_e + piece,
                mine_x,
                other,
            )
        keep(sent_e.at[piece, mine_y], back_ref.at[piece, mine_y], stage_e + piece)
    codes_ref[...] = code_got[pl.ds(mine_x * cols_y, cols_y)]
    for part, (block, begin, some) in enumerate(parts):
        depart(got_a.at[part, pl.ds(0, count - 1), pl.ds(0, 2 * some)], part)
    depart(code_got.at[pl.ds(0, count - 1)], stage_code)
    depart(raw_sent.at[pl.ds(0, cols_y - 1)], stage_raw)
    for piece in range(pieces):
        depart(sent_d.at[piece, pl.ds(0, cols_x - 1)], stage_d + piece)
    arrive(held_ref, stage_raw)
    for piece in range(pieces):
        arrive(back_ref.at[piece], stage_e + piece)
        depart(sent_e.at[piece, pl.ds(0, cols_y - 1)], stage_e + piece)


def encoder(
    features,
    offsets,
    point_cell,
    tile_owner,
    tile_local,
    live_count,
    w_first,
    b_first,
    w_second,
    b_second,
    w_third,
    w_modes,
    z_table,
    backward,
    lift,
):
    cols_x, cols_y = lax.axis_size("gx"), lax.axis_size("gy")
    count = cols_x * cols_y
    own_p, own_q = w_modes.shape[1:3]
    modes, channels = w_modes.shape[0], w_modes.shape[-1]
    hid = w_third.shape[1]
    blocks, listed = tile_owner.shape
    lanes = own_q * channels
    wide = GROUP * hid
    quarter = PB // GROUP
    depth = count * 2 * listed
    slots = modes * 2 * own_p
    smem = pl.BlockSpec(memory_space=pltpu.SMEM)
    vmem = pl.BlockSpec(memory_space=pltpu.VMEM)
    pieces = max(1, lanes // LANES)
    width = lanes // pieces
    anywhere = pl.BlockSpec(memory_space=pl.ANY)
    last = (pieces, cols_y, 2 * CX * CY, width)
    parcel = (pieces, cols_x, 2 * own_p * CX, width)
    number = len(parts_of(blocks, listed))
    stages = number + 2 + 2 * pieces
    return pl.pallas_call(
        encoder_kernel,
        out_shape=(
            jax.ShapeDtypeStruct((cols_y, 8, LANES), jnp.int32),
            jax.ShapeDtypeStruct((cols_y, blocks, quarter, LANES), f32),
            jax.ShapeDtypeStruct(last, f32),
        ),
        in_specs=[smem] * 3 + [vmem] * 9 + [anywhere] * 3,
        out_specs=(vmem, anywhere, anywhere),
        scratch_shapes=[
            pltpu.VMEM(w_modes.shape, w_modes.dtype),
            pltpu.VMEM(backward.shape, backward.dtype),
            pltpu.VMEM(lift.shape, lift.dtype),
            pltpu.VMEM((listed * NZ, 2 * hid), f32),
            pltpu.VMEM((listed * NZ, 2 * hid), f32),
            pltpu.VMEM((quarter, wide), f32),
            pltpu.VMEM((quarter, wide), f32),
            pltpu.VMEM((wide, wide), bf16),
            pltpu.VMEM((UNROLL * wide, 2 * GROUP * channels), bf16),
            pltpu.VMEM((quarter, GROUP * channels), f32),
            pltpu.VMEM((listed * NZ, UNROLL * wide), bf16),
            pltpu.VMEM((listed * NZ, 2 * GROUP * channels), f32),
            pltpu.VMEM((listed, quarter, LANES), f32),
            pltpu.VMEM((8, LANES), jnp.int32),
            pltpu.VMEM((count, 8, LANES), jnp.int32),
            pltpu.VMEM((number, cols_y, 2 * listed, lanes), f32),
            pltpu.VMEM((number, count, 2 * listed, lanes), f32),
            pltpu.VMEM((cols_y, blocks, quarter, LANES), f32),
            pltpu.VMEM((slots, blocks * 3 * depth), bf16),
            pltpu.VMEM((blocks * 3 * depth, lanes), bf16),
            pltpu.VMEM((slots, lanes), f32),
            pltpu.VMEM((slots, lanes), f32),
            pltpu.VMEM(parcel, f32),
            pltpu.VMEM(parcel, f32),
            pltpu.VMEM(last, f32),
            pltpu.SemaphoreType.DMA((3,)),
            pltpu.SemaphoreType.DMA((stages,)),
            pltpu.SemaphoreType.DMA((stages,)),
        ],
        compiler_params=pltpu.CompilerParams(collective_id=0, has_side_effects=True),
        name="encoder",
    )(
        tile_owner,
        tile_local,
        live_count,
        features,
        offsets,
        point_cell[None],
        w_first.T,
        b_first[None],
        w_second,
        b_second[None],
        w_third,
        z_table,
        backward,
        lift,
        w_modes,
    )


def decoder_kernel(
    codes_ref,
    held_ref,
    back_ref,
    inverse_ref,
    w_point_ref,
    b_point_ref,
    out_ref,
    rolled,
    before,
    done,
    out_sem,
):
    cols_y, blocks, quarter = held_ref.shape[:3]
    channels = w_point_ref.shape[0]
    mine_y = lax.axis_index("gy")
    codes_at = len(parts_of(blocks, GROUP))
    groups = LANES // channels
    pieces, width = back_ref.shape[0], back_ref.shape[3]
    each = width // channels
    bias = jnp.concatenate([b_point_ref[...]] * channels, 0).T[:, 0:1]
    before[...] = jnp.zeros_like(before)
    turned = w_point_ref[...].astype(f32).T.astype(bf16)
    turned = jnp.concatenate([turned, turned], 1)
    items = []
    for source in range(cols_y):
        for block in range(blocks):
            flipped = held_ref[source, block].T
            items.append(
                jnp.concatenate(
                    [flipped[j * channels : (j + 1) * channels] for j in range(groups)], 1
                )
            )
    high, low = halves(jnp.concatenate(items, 1))
    points = matmul(turned, jnp.concatenate([high, low], 0))
    for source in range(cols_y):
        for block in range(blocks):
            tile = codes_ref[source, codes_at + block, mine_y]
            item = source * blocks + block

            @pl.when(tile >= 0)
            def _():
                before[tile] += points[:, item * NZ : (item + 1) * NZ]

    for piece in range(pieces):
        value = back_ref[piece].reshape(cols_y * 2 * CX * CY, width)
        value = jnp.concatenate([value] * (LANES // width), 1)
        for shift in range(groups):
            rolled[piece, shift] = pltpu.roll(value, shift * channels, 1) if shift else value
    spans = 2 * cols_y
    lane = lax.broadcasted_iota(jnp.int32, (spans, LANES), 1) // channels
    root = math.sqrt(2.0 / math.pi)
    moves = []
    for chunk in range(CX * CY // groups):
        rows = []
        for q in range(pieces * each):
            found = jnp.zeros((spans, LANES), f32)
            for j in range(groups):
                piece = rolled[
                    q // each,
                    (j - q % each) % groups,
                    pl.ds(chunk * groups + j, spans, stride=CX * CY),
                    :,
                ]
                found = jnp.where(lane == j, piece, found)
            rows.append(found)
        spectral = lax.dot_general(
            split_rows(jnp.concatenate(rows, 0)),
            inverse_ref[...],
            (((0,), (0,)), ((), ())),
            preferred_element_type=f32,
        )
        for j in range(groups):
            tile = chunk * groups + j
            x = spectral[j * channels : (j + 1) * channels] + (before[tile] + bias)
            half = 0.5 * x
            bent = jnp.tanh(x * (root + (0.044715 * root) * (x * x)))
            done[tile // CY, tile % CY] = half + half * bent
        at = (chunk * groups // CY, pl.ds(chunk * groups % CY, groups))
        move = pltpu.make_async_copy(done.at[at], out_ref.at[at], out_sem.at[chunk])
        move.start()
        moves.append(move)
    for move in moves:
        move.wait()


def decoder(codes, held, back, inverse, w_point, b_point):
    smem = pl.BlockSpec(memory_space=pltpu.SMEM)
    vmem = pl.BlockSpec(memory_space=pltpu.VMEM)
    channels = w_point.shape[0]
    rows = back.shape[1] * back.shape[2]
    shape = (CX, CY, channels, NZ)
    return pl.pallas_call(
        decoder_kernel,
        out_shape=jax.ShapeDtypeStruct(shape, f32),
        in_specs=[smem] + [vmem] * 5,
        out_specs=pl.BlockSpec(memory_space=pl.ANY),
        scratch_shapes=[
            pltpu.VMEM((back.shape[0], LANES // channels, rows, LANES), f32),
            pltpu.VMEM((CX * CY, channels, NZ), f32),
            pltpu.VMEM(shape, f32),
            pltpu.SemaphoreType.DMA((CX * CY * channels // LANES,)),
        ],
        name="decoder",
    )(codes, held, back, inverse, w_point, b_point[None])


def local(
    features,
    offsets,
    point_cell,
    tile_owner,
    tile_local,
    live_count,
    w_first,
    b_first,
    w_second,
    b_second,
    w_third,
    w_point,
    b_point,
    w_modes,
):
    z_table, backward, lift, inverse = tables(
        lax.axis_size("gx"), lax.axis_size("gy"), w_modes.shape[0]
    )
    codes, held, back = encoder(
        features,
        offsets,
        point_cell,
        tile_owner,
        tile_local,
        live_count,
        w_first,
        b_first,
        w_second,
        b_second,
        w_third,
        w_modes,
        z_table,
        backward,
        lift,
    )
    return decoder(codes, held, back, inverse, w_point, b_point)


def solution(mesh):
    placed = (
        P(None, ("gx", "gy")),
        P(None, ("gx", "gy")),
        P(("gx", "gy")),
        P(("gx", "gy"), None),
        P(("gx", "gy"), None),
        P(("gx", "gy")),
        P(),
        P(),
        P(),
        P(),
        P(),
        P(),
        P(),
        P(None, "gx", "gy", None, None, None),
    )
    return jax.shard_map(
        local, mesh=mesh, in_specs=placed, out_specs=P("gx", "gy", None, None), check_vma=False
    )
```

```python
import math

import jax
import numpy as np
import jax.numpy as jnp
from jax import lax
from jax.experimental import pallas as pl
from jax.experimental.pallas import tpu as pltpu
from jax.sharding import PartitionSpec as P

NZ = 128
CX = 4
CY = 8
SPAN = 16
PB = 128
LANES = 128

GROUP = 4
UNROLL = 16

LINEAR = 2.0 * math.sqrt(2.0 / math.pi)
CUBIC = 4.0 * 0.044715 * LINEAR

f32 = jnp.float32
bf16 = jnp.bfloat16


def halves(value):
    high = value.astype(bf16)
    return high, (value - high.astype(f32)).astype(bf16)


def split_rows(value):
    high, low = halves(value)
    return jnp.concatenate([high, low, high], 0)


def split_table(table):
    table = np.asarray(table, np.float32)
    high = table.astype(jnp.bfloat16)
    low = (table - high.astype(np.float32)).astype(jnp.bfloat16)
    return np.concatenate([high, high, low], 1)


def matmul(left, right):
    return jnp.dot(left, right, preferred_element_type=f32)


def tables(cols_x, cols_y, modes):
    size_x, size_y = CX * cols_x, CY * cols_y
    own_p, own_q = modes // cols_x, modes // cols_y
    scale = 1.0 / math.sqrt(size_x * size_y * NZ)

    def frequencies(length):
        order = np.arange(modes)
        return np.where(order < modes // 2, order, length - modes + order)

    def turn(angle):
        cosine, sine = np.cos(angle), np.sin(angle)
        return np.array([[cosine, -sine], [sine, cosine]])

    z_turns = 2 * np.pi * (np.outer(np.arange(modes), np.arange(NZ)) % NZ) / NZ
    waves = np.stack([np.cos(z_turns), -np.sin(z_turns)], 0) * scale
    waves = waves.reshape(2, cols_y, own_q, NZ)
    z_table = waves.transpose(2, 0, 1, 3).reshape(-1, NZ)
    inverse = waves.transpose(2, 1, 0, 3).reshape(-1, NZ)
    inverse = np.asarray(inverse, np.float32)
    high = inverse.astype(jnp.bfloat16)
    low = (inverse - high.astype(np.float32)).astype(jnp.bfloat16)
    inverse = np.concatenate([high, high, low], 0)
    x_turns = 2 * np.pi * (np.outer(frequencies(size_x), np.arange(size_x)) % size_x) / size_x
    backward = turn(x_turns).reshape(2, 2, modes // 4, 4, cols_x, CX)
    backward = np.einsum("srgkdx->dsxgrk", backward).reshape(-1, modes * 2)
    y_turns = 2 * np.pi * (np.outer(frequencies(size_y), np.arange(size_y)) % size_y) / size_y
    lift = turn(y_turns).reshape(2, 2, cols_x, own_p, cols_y, CY)
    lift = np.einsum("srepdy,xX->pdsxyerX", lift, np.eye(CX))
    lift = lift.reshape(own_p, 2 * CX * size_y, -1)
    lift = np.stack([split_table(each) for each in lift], 0)
    return split_table(z_table), split_table(backward), lift, inverse


def parts_of(blocks, listed):
    whole = [(block, 0, listed) for block in range(blocks - 1)]
    half = listed // 2
    return whole + [(blocks - 1, 0, half), (blocks - 1, half, listed - half)]


def encoder_kernel(
    owner_ref,
    local_ref,
    live_ref,
    features_ref,
    offsets_ref,
    cells_ref,
    turned_first_ref,
    b_first_ref,
    w_second_ref,
    b_second_ref,
    w_third_ref,
    z_table_ref,
    backward_hbm,
    lift_hbm,
    modes_ref,
    codes_ref,
    held_ref,
    back_ref,
    weights,
    backward_ref,
    lift_ref,
    cell_sin,
    cell_cos,
    point_sin,
    point_cos,
    spread_two,
    spread_three,
    feats,
    second,
    sums,
    dense,
    code_sent,
    code_got,
    sent_a,
    got_a,
    raw_sent,
    phases,
    splits,
    spectra,
    mixed,
    lifted,
    sent_d,
    got_d,
    sent_e,
    load_sem,
    sends,
    recvs,
):
    cols_x, cols_y = lax.axis_size("gx"), lax.axis_size("gy")
    mine_x, mine_y = lax.axis_index("gx"), lax.axis_index("gy")
    count = cols_x * cols_y
    me = mine_x * cols_y + mine_y
    blocks, listed = owner_ref.shape
    hid = w_second_ref.shape[0]
    channels = w_third_ref.shape[0]
    wide = GROUP * hid
    two = 2 * hid
    quarter = PB // GROUP
    size_x, size_y = CX * cols_x, CY * cols_y
    loads = []
    for index, (source, target) in enumerate(
        ((modes_ref, weights), (backward_hbm, backward_ref), (lift_hbm, lift_ref))
    ):
        load = pltpu.make_async_copy(source, target, load_sem.at[index])
        load.start()
        loads.append(load)

    def around(mine, step, size):
        other = mine + step
        return jnp.where(other >= size, other - size, other)

    near_x = [around(mine_x, step, cols_x) for step in range(cols_x)]
    near_y = [around(mine_y, step, cols_y) for step in range(cols_y)]

    def everyone(body):
        if count <= 32:
            for x in near_x:
                for y in near_y:
                    if x is not near_x[0] or y is not near_y[0]:
                        body(x, y)
        else:

            @pl.loop(1, count)
            def _(step):
                other = lax.rem(me + step, count)
                x = lax.div(other, cols_y)
                body(x, other - x * cols_y)

    barrier = pltpu.get_barrier_semaphore()

    def greet(x, y):
        pl.semaphore_signal(barrier, inc=1, device_id={"gx": x, "gy": y})

    everyone(greet)

    turned_two = (w_second_ref[...].astype(f32).T * 0.5).astype(bf16)
    turned_three = w_third_ref[...].astype(f32).T
    spread_two[...] = jnp.zeros_like(spread_two)
    spread_three[...] = jnp.zeros_like(spread_three)
    for part in range(GROUP):
        rows = slice(part * hid, (part + 1) * hid)
        spread_two[rows, rows] = turned_two
    bias = jnp.concatenate([b_second_ref[...] * 0.5] * GROUP, 1)
    wide_three = jnp.concatenate([turned_three] * GROUP, 1)
    coarse_y, coarse_z = size_y // SPAN, NZ // SPAN
    cells = cells_ref[...]
    coarse = jnp.concatenate(
        [cells // (coarse_y * coarse_z), cells // coarse_z % coarse_y, cells % coarse_z], 0
    )
    places = coarse.astype(f32) * SPAN + offsets_ref[...].astype(f32)
    places = jnp.concatenate([places, jnp.zeros((5, places.shape[1]), f32)], 0)
    turned_first = turned_first_ref[...].astype(f32)
    double_first = jnp.concatenate([turned_first, turned_first], 1)
    features = features_ref[...].astype(f32)

    steps = lax.broadcasted_iota(jnp.int32, (24, two), 0)
    steps = jnp.where(steps < 16, steps * 8, steps - 16).astype(f32)
    steps = steps * double_first[2:3]
    cosine, sine = jnp.cos(steps), jnp.sin(steps)
    cos_fine, sin_fine = cosine[16:24], sine[16:24]
    bases = []
    for block in range(blocks):
        for slot in range(listed):
            tile = local_ref[block, slot]
            cell_x = (CX * mine_x + tile // CY).astype(f32)
            cell_y = (CY * owner_ref[block, slot] + tile % CY).astype(f32)
            bases.append(
                turned_first[0:1] * cell_x + turned_first[1:2] * cell_y + b_first_ref[...]
            )
    base = jnp.concatenate(bases, 0)
    base = jnp.concatenate([base, base], 1)
    base_sin, base_cos = jnp.sin(base), jnp.cos(base)
    code_lane = lax.broadcasted_iota(jnp.int32, (1, LANES), 1)
    code_rows = []
    parts = parts_of(blocks, listed)
    for block, begin, some in parts:
        row = jnp.zeros((1, LANES), jnp.int32)
        for slot in range(some):
            code = (
                owner_ref[block, begin + slot] * (CX * CY) + local_ref[block, begin + slot]
            )
            row = jnp.where(code_lane % some == slot, code, row)
        code_rows.append(row)
    for block in range(blocks):
        row = jnp.full((1, LANES), -1, jnp.int32)
        for slot in range(listed):
            alive = jnp.where(slot < live_ref[block], local_ref[block, slot], -1)
            row = jnp.where(code_lane == owner_ref[block, slot], alive, row)
        code_rows.append(row)
    code_rows.append(jnp.zeros((8 - len(code_rows), LANES), jnp.int32))
    code_sent[...] = jnp.concatenate(code_rows, 0)

    lane = lax.broadcasted_iota(jnp.int32, (quarter, two), 1)

    def points(block):
        here = slice(block * PB, (block + 1) * PB)
        spots = places[:, here].T
        for half in range(GROUP // 2):
            low = slice(2 * half * quarter, (2 * half + 1) * quarter)
            up = slice((2 * half + 1) * quarter, (2 * half + 2) * quarter)
            cols = slice(half * two, (half + 1) * two)
            side = 0.0
            for axis in range(3):
                spot = jnp.where(lane < hid, spots[low, axis : axis + 1], spots[up, axis : axis + 1])
                side = side + double_first[axis : axis + 1] * spot
            point_cos[:, cols] = jnp.cos(side)
            point_sin[:, cols] = jnp.sin(side)
        turned = features[:, here].T
        feats[...] = jnp.concatenate(
            [turned[j * quarter : (j + 1) * quarter] for j in range(GROUP)], 1
        )

    def pairs(block, begin, some):
        for slot in range(some):
            item = block * listed + begin + slot
            b_sin, b_cos = base_sin[item : item + 1], base_cos[item : item + 1]
            near_sin = sin_fine * b_cos + cos_fine * b_sin
            near_cos = cos_fine * b_cos - sin_fine * b_sin
            for step in range(NZ // 8):
                rows = slice(slot * NZ + step * 8, slot * NZ + step * 8 + 8)
                far_cos, far_sin = cosine[step : step + 1], sine[step : step + 1]
                cell_sin[rows, :] = far_cos * near_sin + far_sin * near_cos
                cell_cos[rows, :] = far_cos * near_cos - far_sin * near_sin
        sums[...] = jnp.zeros_like(sums)

        @pl.loop(0, quarter // UNROLL)
        def _(step):
            for inner in range(UNROLL):
                weigh = wide_three * feats[pl.ds(step * UNROLL + inner, 1), :]
                high, rest = halves(weigh)
                for part in range(GROUP):
                    rows = slice(inner * wide + part * hid, inner * wide + (part + 1) * hid)
                    cols = slice(part * channels, (part + 1) * channels)
                    spread_three[rows, part * channels : (part + 1) * channels] = high[:, cols]
                    spread_three[
                        rows, LANES + part * channels : LANES + (part + 1) * channels
                    ] = rest[:, cols]
            for slot in range(some):
                rows = slice(slot * NZ, (slot + 1) * NZ)
                for inner in range(UNROLL):
                    group = step * UNROLL + inner
                    p_cos, p_sin = point_cos[pl.ds(group, 1), :], point_sin[pl.ds(group, 1), :]
                    c_sin, c_cos = cell_sin[rows, :], cell_cos[rows, :]
                    hidden = []
                    for half in range(GROUP // 2):
                        cols = slice(half * two, (half + 1) * two)
                        value = c_sin * p_cos[:, cols] - c_cos * p_sin[:, cols]
                        hidden.append(value.astype(bf16))
                    y = matmul(jnp.concatenate(hidden, 1), spread_two[...]) + bias
                    bent = jnp.tanh(y * (LINEAR + CUBIC * (y * y)))
                    second[rows, inner * wide : (inner + 1) * wide] = (y + y * bent).astype(bf16)
                sums[rows, :] += matmul(second[rows, :], spread_three[...])

    own_q = sent_a.shape[3] // channels
    lane_z = lax.broadcasted_iota(jnp.int32, (NZ, LANES), 1) // channels
    lane_r = lax.broadcasted_iota(jnp.int32, (quarter, LANES), 1) // channels
    scale = 1.0 / math.sqrt(PB)

    def parcels(part):
        block, begin, some = parts[part]
        flat = jnp.zeros((NZ, LANES), f32)
        for slot in range(some):
            rows = slice(slot * NZ, (slot + 1) * NZ)
            total = sums[rows, 0:LANES] + sums[rows, LANES:]
            total = total + pltpu.roll(total, 2 * channels, 1)
            total = total + pltpu.roll(total, channels, 1)
            total = jnp.where(begin + slot < live_ref[block], total * scale, 0.0)
            flat = jnp.where(lane_z == slot, total, flat)
            tight = total[0:quarter]
            for at in range(1, GROUP):
                tight = jnp.where(lane_r == at, total[at * quarter : (at + 1) * quarter], tight)
            dense[begin + slot] = tight
        modes = matmul(z_table_ref[...], split_rows(flat))
        span = 2 * cols_y
        for slot in range(some):
            lanes = slice(slot * channels, (slot + 1) * channels)
            joined = jnp.concatenate(
                [modes[q * span : (q + 1) * span, lanes] for q in range(own_q)], 1
            )
            for half in range(2):
                sent_a[part, :, half * some + slot, :] = joined[
                    half * cols_y : (half + 1) * cols_y
                ]

    def raws(block):
        for dest in range(cols_y):
            chosen = jnp.zeros((quarter, LANES), f32)
            for slot in range(listed):
                chosen = jnp.where(owner_ref[block, slot] == dest, dense[slot], chosen)
            raw_sent[dest, block] = chosen

    def send(source, target, stage, x, y):
        pltpu.make_async_remote_copy(
            src_ref=source,
            dst_ref=target,
            send_sem=sends.at[stage],
            recv_sem=recvs.at[stage],
            device_id={"gx": x, "gy": y},
        ).start()

    def keep(source, target, stage):
        pltpu.make_async_copy(source, target, recvs.at[stage]).start()

    def spread(part):
        rows = pl.ds(0, 2 * parts[part][2])

        def go(x, y):
            send(sent_a.at[part, y, rows], got_a.at[part, me, rows], part, x, y)

        everyone(go)
        keep(sent_a.at[part, mine_y, rows], got_a.at[part, me, rows], part)

    def arrive(target, stage):
        pltpu.make_async_copy(target, target, recvs.at[stage]).wait()

    def depart(part, stage):
        pltpu.make_async_copy(part, part, sends.at[stage]).wait()

    stage_code = len(parts)
    stage_raw, stage_d = stage_code + 1, stage_code + 2
    stage_e = stage_d + sent_d.shape[0]

    for part, (block, begin, some) in enumerate(parts):
        if begin == 0:
            points(block)
        pairs(block, begin, some)
        parcels(part)
        if part == 0:
            pl.semaphore_wait(barrier, count - 1)

            def tell(x, y):
                send(code_sent, code_got.at[me], stage_code, x, y)

            everyone(tell)
            keep(code_sent, code_got.at[me], stage_code)
        spread(part)
        if begin + some == listed:
            raws(block)

    arrive(code_got, stage_code)
    own_p = sent_d.shape[0]
    modes = own_p * cols_x
    slots = modes * 2
    lanes_w = got_a.shape[3]

    def waves(turns):
        angle = (turns - jnp.floor(turns)) * (2.0 * math.pi)
        return jnp.cos(angle), jnp.sin(angle)

    starts = [0]
    for part, (block, begin, some) in enumerate(parts):
        each = 2 * some
        depth = count * each
        column = lax.broadcasted_iota(jnp.int32, (1, depth), 1)
        source = column // each
        row = lax.broadcasted_iota(jnp.int32, (slots, depth), 0)
        which = (row // 8) * 4 + row % 4
        freq_x = jnp.where(which < modes // 2, which, size_x - modes + which)
        part_out = (row // 4) % 2
        part_in = (column // some) % 2
        quarters = (part_out - part_in).astype(f32) * 0.25
        p_at = mine_x * own_p + lax.broadcasted_iota(jnp.int32, (own_p, depth), 0)
        freq_y = jnp.where(p_at < modes // 2, p_at, size_y - modes + p_at)
        owns = (
            lax.broadcasted_iota(jnp.int32, (count, depth), 1) // each
            == lax.broadcasted_iota(jnp.int32, (count, depth), 0)
        )
        codes = jnp.concatenate([code_got[:, part, :].astype(f32)] * (depth // LANES), 1)
        code = jnp.sum(jnp.where(owns, codes, 0.0), axis=0, keepdims=True).astype(jnp.int32)
        tile = code % (CX * CY)
        x_at = CX * (source // cols_y) + tile // CY
        y_at = CY * (code // (CX * CY)) + tile % CY
        x_cos, x_sin = waves((freq_x * x_at).astype(f32) * (1.0 / size_x) + quarters)
        y_cos, y_sin = waves((freq_y * y_at).astype(f32) * (1.0 / size_y))
        start = starts[part]
        for p in range(own_p):
            value = x_cos * y_cos[p : p + 1] - x_sin * y_sin[p : p + 1]
            high, low = halves(value)
            rows = slice(p * slots, (p + 1) * slots)
            phases[rows, start : start + depth] = high
            phases[rows, start + depth : start + 2 * depth] = high
            phases[rows, start + 2 * depth : start + 3 * depth] = low
        starts.append(start + 3 * depth)
    for part, (block, begin, some) in enumerate(parts):
        rows = pl.ds(0, 2 * some)
        arrive(got_a.at[part, :, rows], part)
        splits[starts[part] : starts[part + 1], :] = split_rows(
            got_a[part, :, 0 : 2 * some].reshape(count * 2 * some, lanes_w)
        )
        if part == len(parts) - 2:
            seen = slice(0, starts[part + 1])
            spectra[...] = matmul(phases[:, seen], splits[seen, :])
    seen = slice(starts[-2], starts[-1])
    spectra[...] += matmul(phases[:, seen], splits[seen, :])

    for step in range(1, cols_y):
        other = near_y[step]
        send(raw_sent.at[other], held_ref.at[mine_y], stage_raw, mine_x, other)
    keep(raw_sent.at[mine_y], held_ref.at[mine_y], stage_raw)

    for load in loads:
        load.wait()
    quad = 8 * channels
    bands = LANES // channels
    row_of = lax.broadcasted_iota(jnp.int32, (8, LANES), 0)
    lane_of = lax.broadcasted_iota(jnp.int32, (8, LANES), 1)
    band = lane_of // channels
    own_four = [row_of % 4 == 2 * side + lane_of // (2 * channels) for side in range(2)]
    negate = row_of < 4
    fours = modes // 4
    tiles = max(1, lanes_w // LANES)
    width = lanes_w // tiles
    each = width // channels
    for p in range(own_p):
        for group in range(fours):
            rows = slice((p * fours + group) * 8, (p * fours + group) * 8 + 8)
            for at_tile in range(tiles):
                cols = slice(at_tile * width, (at_tile + 1) * width)
                plain = jnp.concatenate([spectra[rows, cols]] * (LANES // width), 1)
                turned = pltpu.roll(plain, 4, 0)
                turned = jnp.where(negate, -turned, turned)
                plains = [plain] + [pltpu.roll(plain, r * channels, 1) for r in range(1, bands)]
                turns = [turned] + [pltpu.roll(turned, r * channels, 1) for r in range(1, bands)]
                outs = []
                for q in range(each):
                    both = plains[-q % bands]
                    for at in range(1, bands):
                        kind = turns if at % 2 else plains
                        both = jnp.where(band == at, kind[(at - q) % bands], both)
                    both = jnp.concatenate([jnp.where(own, both, 0.0) for own in own_four], 1)
                    high, rest = halves(both)
                    tile = weights[group * 4 : group * 4 + 4, p, at_tile * each + q]
                    out = matmul(jnp.concatenate([high, rest], 0), tile.reshape(quad, channels))
                    outs.append(out[:8] + out[8:])
                mixed[group * 8 : group * 8 + 8, cols] = jnp.concatenate(outs, 1)
        along_x = matmul(backward_ref[...], split_rows(mixed[...]))
        sent_d[p] = along_x.reshape(sent_d.shape[1:])
        for step in range(1, cols_x):
            other = near_x[step]
            send(sent_d.at[p, other], got_d.at[p, mine_x], stage_d + p, other, mine_y)
        keep(sent_d.at[p, mine_x], got_d.at[p, mine_x], stage_d + p)
    for p in range(own_p - 1):
        arrive(got_d.at[p], stage_d + p)
        part = matmul(lift_ref[p], split_rows(got_d[p].reshape(-1, lanes_w)))
        lifted[...] = part if p == 0 else lifted[...] + part
    p = own_p - 1
    arrive(got_d.at[p], stage_d + p)
    for piece in range(tiles):
        cols = slice(piece * width, (piece + 1) * width)
        along_y = matmul(lift_ref[p], split_rows(got_d[p, :, :, cols].reshape(-1, width)))
        if p:
            along_y = lifted[:, cols] + along_y
        sent_e[piece] = along_y.reshape(sent_e.shape[1:])
        for step in range(1, cols_y):
            other = near_y[step]
            send(
                sent_e.at[piece, other],
                back_ref.at[piece, mine_y],
                stage_e + piece,
                mine_x,
                other,
            )
        keep(sent_e.at[piece, mine_y], back_ref.at[piece, mine_y], stage_e + piece)
    codes_ref[...] = code_got[pl.ds(mine_x * cols_y, cols_y)]
    for part, (block, begin, some) in enumerate(parts):
        depart(got_a.at[part, pl.ds(0, count - 1), pl.ds(0, 2 * some)], part)
    depart(code_got.at[pl.ds(0, count - 1)], stage_code)
    depart(raw_sent.at[pl.ds(0, cols_y - 1)], stage_raw)
    for p in range(own_p):
        depart(sent_d.at[p, pl.ds(0, cols_x - 1)], stage_d + p)
    arrive(held_ref, stage_raw)
    for piece in range(tiles):
        arrive(back_ref.at[piece], stage_e + piece)
        depart(sent_e.at[piece, pl.ds(0, cols_y - 1)], stage_e + piece)


def encoder(
    features,
    offsets,
    point_cell,
    tile_owner,
    tile_local,
    live_count,
    w_first,
    b_first,
    w_second,
    b_second,
    w_third,
    w_modes,
    z_table,
    backward,
    lift,
):
    cols_x, cols_y = lax.axis_size("gx"), lax.axis_size("gy")
    count = cols_x * cols_y
    own_p, own_q = w_modes.shape[1:3]
    modes, channels = w_modes.shape[0], w_modes.shape[-1]
    hid = w_third.shape[1]
    blocks, listed = tile_owner.shape
    lanes = own_q * channels
    wide = GROUP * hid
    quarter = PB // GROUP
    depth = count * 2 * listed
    slots = modes * 2 * own_p
    smem = pl.BlockSpec(memory_space=pltpu.SMEM)
    vmem = pl.BlockSpec(memory_space=pltpu.VMEM)
    pieces = max(1, lanes // LANES)
    width = lanes // pieces
    anywhere = pl.BlockSpec(memory_space=pl.ANY)
    last = (pieces, cols_y, 2 * CX * CY, width)
    parcel = (own_p, cols_x, 2 * CX, lanes)
    number = len(parts_of(blocks, listed))
    stages = number + 2 + own_p + pieces
    return pl.pallas_call(
        encoder_kernel,
        out_shape=(
            jax.ShapeDtypeStruct((cols_y, 8, LANES), jnp.int32),
            jax.ShapeDtypeStruct((cols_y, blocks, quarter, LANES), f32),
            jax.ShapeDtypeStruct(last, f32),
        ),
        in_specs=[smem] * 3 + [vmem] * 9 + [anywhere] * 3,
        out_specs=(vmem, anywhere, anywhere),
        scratch_shapes=[
            pltpu.VMEM(w_modes.shape, w_modes.dtype),
            pltpu.VMEM(backward.shape, backward.dtype),
            pltpu.VMEM(lift.shape, lift.dtype),
            pltpu.VMEM((listed * NZ, 2 * hid), f32),
            pltpu.VMEM((listed * NZ, 2 * hid), f32),
            pltpu.VMEM((quarter, wide), f32),
            pltpu.VMEM((quarter, wide), f32),
            pltpu.VMEM((wide, wide), bf16),
            pltpu.VMEM((UNROLL * wide, 2 * GROUP * channels), bf16),
            pltpu.VMEM((quarter, GROUP * channels), f32),
            pltpu.VMEM((listed * NZ, UNROLL * wide), bf16),
            pltpu.VMEM((listed * NZ, 2 * GROUP * channels), f32),
            pltpu.VMEM((listed, quarter, LANES), f32),
            pltpu.VMEM((8, LANES), jnp.int32),
            pltpu.VMEM((count, 8, LANES), jnp.int32),
            pltpu.VMEM((number, cols_y, 2 * listed, lanes), f32),
            pltpu.VMEM((number, count, 2 * listed, lanes), f32),
            pltpu.VMEM((cols_y, blocks, quarter, LANES), f32),
            pltpu.VMEM((slots, blocks * 3 * depth), bf16),
            pltpu.VMEM((blocks * 3 * depth, lanes), bf16),
            pltpu.VMEM((slots, lanes), f32),
            pltpu.VMEM((modes * 2, lanes), f32),
            pltpu.VMEM((lift.shape[1], lanes), f32),
            pltpu.VMEM(parcel, f32),
            pltpu.VMEM(parcel, f32),
            pltpu.VMEM(last, f32),
            pltpu.SemaphoreType.DMA((3,)),
            pltpu.SemaphoreType.DMA((stages,)),
            pltpu.SemaphoreType.DMA((stages,)),
        ],
        compiler_params=pltpu.CompilerParams(collective_id=0, has_side_effects=True),
        name="encoder",
    )(
        tile_owner,
        tile_local,
        live_count,
        features,
        offsets,
        point_cell[None],
        w_first.T,
        b_first[None],
        w_second,
        b_second[None],
        w_third,
        z_table,
        backward,
        lift,
        w_modes,
    )


def decoder_kernel(
    codes_ref,
    held_ref,
    back_ref,
    inverse_ref,
    w_point_ref,
    b_point_ref,
    out_ref,
    rolled,
    before,
    done,
    out_sem,
):
    cols_y, blocks, quarter = held_ref.shape[:3]
    channels = w_point_ref.shape[0]
    mine_y = lax.axis_index("gy")
    codes_at = len(parts_of(blocks, GROUP))
    groups = LANES // channels
    pieces, width = back_ref.shape[0], back_ref.shape[3]
    each = width // channels
    bias = jnp.concatenate([b_point_ref[...]] * channels, 0).T[:, 0:1]
    before[...] = jnp.zeros_like(before)
    turned = w_point_ref[...].astype(f32).T.astype(bf16)
    turned = jnp.concatenate([turned, turned], 1)
    items = []
    for source in range(cols_y):
        for block in range(blocks):
            flipped = held_ref[source, block].T
            items.append(
                jnp.concatenate(
                    [flipped[j * channels : (j + 1) * channels] for j in range(groups)], 1
                )
            )
    high, low = halves(jnp.concatenate(items, 1))
    points = matmul(turned, jnp.concatenate([high, low], 0))
    for source in range(cols_y):
        for block in range(blocks):
            tile = codes_ref[source, codes_at + block, mine_y]
            item = source * blocks + block

            @pl.when(tile >= 0)
            def _():
                before[tile] += points[:, item * NZ : (item + 1) * NZ]

    for piece in range(pieces):
        value = back_ref[piece].reshape(cols_y * 2 * CX * CY, width)
        value = jnp.concatenate([value] * (LANES // width), 1)
        for shift in range(groups):
            rolled[piece, shift] = pltpu.roll(value, shift * channels, 1) if shift else value
    spans = 2 * cols_y
    lane = lax.broadcasted_iota(jnp.int32, (spans, LANES), 1) // channels
    root = math.sqrt(2.0 / math.pi)
    moves = []
    for chunk in range(CX * CY // groups):
        rows = []
        for q in range(pieces * each):
            found = jnp.zeros((spans, LANES), f32)
            for j in range(groups):
                piece = rolled[
                    q // each,
                    (j - q % each) % groups,
                    pl.ds(chunk * groups + j, spans, stride=CX * CY),
                    :,
                ]
                found = jnp.where(lane == j, piece, found)
            rows.append(found)
        spectral = lax.dot_general(
            split_rows(jnp.concatenate(rows, 0)),
            inverse_ref[...],
            (((0,), (0,)), ((), ())),
            preferred_element_type=f32,
        )
        for j in range(groups):
            tile = chunk * groups + j
            x = spectral[j * channels : (j + 1) * channels] + (before[tile] + bias)
            half = 0.5 * x
            bent = jnp.tanh(x * (root + (0.044715 * root) * (x * x)))
            done[tile // CY, tile % CY] = half + half * bent
        at = (chunk * groups // CY, pl.ds(chunk * groups % CY, groups))
        move = pltpu.make_async_copy(done.at[at], out_ref.at[at], out_sem.at[chunk])
        move.start()
        moves.append(move)
    for move in moves:
        move.wait()


def decoder(codes, held, back, inverse, w_point, b_point):
    smem = pl.BlockSpec(memory_space=pltpu.SMEM)
    vmem = pl.BlockSpec(memory_space=pltpu.VMEM)
    channels = w_point.shape[0]
    rows = back.shape[1] * back.shape[2]
    shape = (CX, CY, channels, NZ)
    return pl.pallas_call(
        decoder_kernel,
        out_shape=jax.ShapeDtypeStruct(shape, f32),
        in_specs=[smem] + [vmem] * 5,
        out_specs=pl.BlockSpec(memory_space=pl.ANY),
        scratch_shapes=[
            pltpu.VMEM((back.shape[0], LANES // channels, rows, LANES), f32),
            pltpu.VMEM((CX * CY, channels, NZ), f32),
            pltpu.VMEM(shape, f32),
            pltpu.SemaphoreType.DMA((CX * CY * channels // LANES,)),
        ],
        name="decoder",
    )(codes, held, back, inverse, w_point, b_point[None])


def local(
    features,
    offsets,
    point_cell,
    tile_owner,
    tile_local,
    live_count,
    w_first,
    b_first,
    w_second,
    b_second,
    w_third,
    w_point,
    b_point,
    w_modes,
):
    z_table, backward, lift, inverse = tables(
        lax.axis_size("gx"), lax.axis_size("gy"), w_modes.shape[0]
    )
    codes, held, back = encoder(
        features,
        offsets,
        point_cell,
        tile_owner,
        tile_local,
        live_count,
        w_first,
        b_first,
        w_second,
        b_second,
        w_third,
        w_modes,
        z_table,
        backward,
        lift,
    )
    return decoder(codes, held, back, inverse, w_point, b_point)


def solution(mesh):
    placed = (
        P(None, ("gx", "gy")),
        P(None, ("gx", "gy")),
        P(("gx", "gy")),
        P(("gx", "gy"), None),
        P(("gx", "gy"), None),
        P(("gx", "gy")),
        P(),
        P(),
        P(),
        P(),
        P(),
        P(),
        P(),
        P(None, "gx", "gy", None, None, None),
    )
    return jax.shard_map(
        local, mesh=mesh, in_specs=placed, out_specs=P("gx", "gy", None, None), check_vma=False
    )
```

```python
import math

import jax
import numpy as np
import jax.numpy as jnp
from jax import lax
from jax.experimental import pallas as pl
from jax.experimental.pallas import tpu as pltpu
from jax.sharding import PartitionSpec as P

NZ = 128
CX = 4
CY = 8
SPAN = 16
PB = 128
LANES = 128

GROUP = 4
UNROLL = 16

LINEAR = 2.0 * math.sqrt(2.0 / math.pi)
CUBIC = 4.0 * 0.044715 * LINEAR

f32 = jnp.float32
bf16 = jnp.bfloat16


def halves(value):
    high = value.astype(bf16)
    return high, (value - high.astype(f32)).astype(bf16)


def split_rows(value):
    high, low = halves(value)
    return jnp.concatenate([high, low, high], 0)


def split_table(table):
    table = np.asarray(table, np.float32)
    high = table.astype(jnp.bfloat16)
    low = (table - high.astype(np.float32)).astype(jnp.bfloat16)
    return np.concatenate([high, high, low], 1)


def matmul(left, right):
    return jnp.dot(left, right, preferred_element_type=f32)


def tables(cols_x, cols_y, modes):
    size_x, size_y = CX * cols_x, CY * cols_y
    own_p, own_q = modes // cols_x, modes // cols_y
    scale = 1.0 / math.sqrt(size_x * size_y * NZ)

    def frequencies(length):
        order = np.arange(modes)
        return np.where(order < modes // 2, order, length - modes + order)

    def turn(angle):
        cosine, sine = np.cos(angle), np.sin(angle)
        return np.array([[cosine, -sine], [sine, cosine]])

    z_turns = 2 * np.pi * (np.outer(np.arange(modes), np.arange(NZ)) % NZ) / NZ
    waves = np.stack([np.cos(z_turns), -np.sin(z_turns)], 0) * scale
    waves = waves.reshape(2, cols_y, own_q, NZ)
    z_table = waves.transpose(2, 0, 1, 3).reshape(-1, NZ)
    inverse = waves.transpose(2, 1, 0, 3).reshape(-1, NZ)
    inverse = np.asarray(inverse, np.float32)
    high = inverse.astype(jnp.bfloat16)
    low = (inverse - high.astype(np.float32)).astype(jnp.bfloat16)
    inverse = np.concatenate([high, high, low], 0)
    x_turns = 2 * np.pi * (np.outer(frequencies(size_x), np.arange(size_x)) % size_x) / size_x
    backward = turn(x_turns).reshape(2, 2, modes // 4, 4, cols_x, CX)
    backward = np.einsum("srgkdx->dsxgrk", backward).reshape(-1, modes * 2)
    y_turns = 2 * np.pi * (np.outer(frequencies(size_y), np.arange(size_y)) % size_y) / size_y
    lift = turn(y_turns).reshape(2, 2, cols_x, own_p, cols_y, CY)
    lift = np.einsum("srepdy,xX->pdsxyerX", lift, np.eye(CX))
    lift = lift.reshape(own_p, 2 * CX * size_y, -1)
    lift = np.stack([split_table(each) for each in lift], 0)
    return split_table(z_table), split_table(backward), lift, inverse


def parts_of(blocks, listed):
    whole = [(block, 0, listed) for block in range(blocks - 1)]
    half = listed // 2
    return whole + [(blocks - 1, 0, half), (blocks - 1, half, listed - half)]


def encoder_kernel(
    owner_ref,
    local_ref,
    live_ref,
    features_ref,
    offsets_ref,
    cells_ref,
    turned_first_ref,
    b_first_ref,
    w_second_ref,
    b_second_ref,
    w_third_ref,
    z_table_ref,
    backward_hbm,
    lift_hbm,
    modes_ref,
    codes_ref,
    held_ref,
    back_ref,
    weights,
    backward_ref,
    lift_ref,
    cell_sin,
    cell_cos,
    point_sin,
    point_cos,
    spread_two,
    spread_three,
    feats,
    second,
    sums,
    dense,
    code_sent,
    code_got,
    sent_a,
    got_a,
    sent_b,
    got_b,
    raw_sent,
    phases,
    splits,
    spectra,
    mixed,
    lifted,
    sent_d,
    got_d,
    sent_e,
    load_sem,
    sends,
    recvs,
):
    cols_x, cols_y = lax.axis_size("gx"), lax.axis_size("gy")
    mine_x, mine_y = lax.axis_index("gx"), lax.axis_index("gy")
    count = cols_x * cols_y
    me = mine_x * cols_y + mine_y
    blocks, listed = owner_ref.shape
    hid = w_second_ref.shape[0]
    channels = w_third_ref.shape[0]
    wide = GROUP * hid
    two = 2 * hid
    quarter = PB // GROUP
    size_x, size_y = CX * cols_x, CY * cols_y
    loads = []
    for index, (source, target) in enumerate(
        ((modes_ref, weights), (backward_hbm, backward_ref), (lift_hbm, lift_ref))
    ):
        load = pltpu.make_async_copy(source, target, load_sem.at[index])
        load.start()
        loads.append(load)

    def around(mine, step, size):
        other = mine + step
        return jnp.where(other >= size, other - size, other)

    near_x = [around(mine_x, step, cols_x) for step in range(cols_x)]
    near_y = [around(mine_y, step, cols_y) for step in range(cols_y)]

    def everyone(body):
        if count <= 32:
            for x in near_x:
                for y in near_y:
                    if x is not near_x[0] or y is not near_y[0]:
                        body(x, y)
        else:

            @pl.loop(1, count)
            def _(step):
                other = lax.rem(me + step, count)
                x = lax.div(other, cols_y)
                body(x, other - x * cols_y)

    barrier = pltpu.get_barrier_semaphore()

    def greet(x, y):
        pl.semaphore_signal(barrier, inc=1, device_id={"gx": x, "gy": y})

    everyone(greet)

    turned_two = (w_second_ref[...].astype(f32).T * 0.5).astype(bf16)
    turned_three = w_third_ref[...].astype(f32).T
    spread_two[...] = jnp.zeros_like(spread_two)
    spread_three[...] = jnp.zeros_like(spread_three)
    for part in range(GROUP):
        rows = slice(part * hid, (part + 1) * hid)
        spread_two[rows, rows] = turned_two
    bias = jnp.concatenate([b_second_ref[...] * 0.5] * GROUP, 1)
    wide_three = jnp.concatenate([turned_three] * GROUP, 1)
    coarse_y, coarse_z = size_y // SPAN, NZ // SPAN
    cells = cells_ref[...]
    coarse = jnp.concatenate(
        [cells // (coarse_y * coarse_z), cells // coarse_z % coarse_y, cells % coarse_z], 0
    )
    places = coarse.astype(f32) * SPAN + offsets_ref[...].astype(f32)
    places = jnp.concatenate([places, jnp.zeros((5, places.shape[1]), f32)], 0)
    turned_first = turned_first_ref[...].astype(f32)
    double_first = jnp.concatenate([turned_first, turned_first], 1)
    features = features_ref[...].astype(f32)

    steps = lax.broadcasted_iota(jnp.int32, (24, two), 0)
    steps = jnp.where(steps < 16, steps * 8, steps - 16).astype(f32)
    steps = steps * double_first[2:3]
    cosine, sine = jnp.cos(steps), jnp.sin(steps)
    cos_fine, sin_fine = cosine[16:24], sine[16:24]
    bases = []
    for block in range(blocks):
        for slot in range(listed):
            tile = local_ref[block, slot]
            cell_x = (CX * mine_x + tile // CY).astype(f32)
            cell_y = (CY * owner_ref[block, slot] + tile % CY).astype(f32)
            bases.append(
                turned_first[0:1] * cell_x + turned_first[1:2] * cell_y + b_first_ref[...]
            )
    base = jnp.concatenate(bases, 0)
    base = jnp.concatenate([base, base], 1)
    base_sin, base_cos = jnp.sin(base), jnp.cos(base)
    code_lane = lax.broadcasted_iota(jnp.int32, (1, LANES), 1)
    code_rows = []
    parts = parts_of(blocks, listed)
    for block, begin, some in parts:
        row = jnp.zeros((1, LANES), jnp.int32)
        for slot in range(some):
            code = (
                owner_ref[block, begin + slot] * (CX * CY) + local_ref[block, begin + slot]
            )
            row = jnp.where(code_lane % some == slot, code, row)
        code_rows.append(row)
    for block in range(blocks):
        row = jnp.full((1, LANES), -1, jnp.int32)
        for slot in range(listed):
            alive = jnp.where(slot < live_ref[block], local_ref[block, slot], -1)
            row = jnp.where(code_lane == owner_ref[block, slot], alive, row)
        code_rows.append(row)
    code_rows.append(jnp.zeros((8 - len(code_rows), LANES), jnp.int32))
    code_sent[...] = jnp.concatenate(code_rows, 0)

    lane = lax.broadcasted_iota(jnp.int32, (quarter, two), 1)

    def points(block):
        here = slice(block * PB, (block + 1) * PB)
        spots = places[:, here].T
        for half in range(GROUP // 2):
            low = slice(2 * half * quarter, (2 * half + 1) * quarter)
            up = slice((2 * half + 1) * quarter, (2 * half + 2) * quarter)
            cols = slice(half * two, (half + 1) * two)
            side = 0.0
            for axis in range(3):
                spot = jnp.where(lane < hid, spots[low, axis : axis + 1], spots[up, axis : axis + 1])
                side = side + double_first[axis : axis + 1] * spot
            point_cos[:, cols] = jnp.cos(side)
            point_sin[:, cols] = jnp.sin(side)
        turned = features[:, here].T
        feats[...] = jnp.concatenate(
            [turned[j * quarter : (j + 1) * quarter] for j in range(GROUP)], 1
        )

    def pairs(block, begin, some):
        for slot in range(some):
            item = block * listed + begin + slot
            b_sin, b_cos = base_sin[item : item + 1], base_cos[item : item + 1]
            near_sin = sin_fine * b_cos + cos_fine * b_sin
            near_cos = cos_fine * b_cos - sin_fine * b_sin
            for step in range(NZ // 8):
                rows = slice(slot * NZ + step * 8, slot * NZ + step * 8 + 8)
                far_cos, far_sin = cosine[step : step + 1], sine[step : step + 1]
                cell_sin[rows, :] = far_cos * near_sin + far_sin * near_cos
                cell_cos[rows, :] = far_cos * near_cos - far_sin * near_sin
        sums[...] = jnp.zeros_like(sums)

        @pl.loop(0, quarter // UNROLL)
        def _(step):
            for inner in range(UNROLL):
                weigh = wide_three * feats[pl.ds(step * UNROLL + inner, 1), :]
                high, rest = halves(weigh)
                for part in range(GROUP):
                    rows = slice(inner * wide + part * hid, inner * wide + (part + 1) * hid)
                    cols = slice(part * channels, (part + 1) * channels)
                    spread_three[rows, part * channels : (part + 1) * channels] = high[:, cols]
                    spread_three[
                        rows, LANES + part * channels : LANES + (part + 1) * channels
                    ] = rest[:, cols]
            for slot in range(some):
                rows = slice(slot * NZ, (slot + 1) * NZ)
                for inner in range(UNROLL):
                    group = step * UNROLL + inner
                    p_cos, p_sin = point_cos[pl.ds(group, 1), :], point_sin[pl.ds(group, 1), :]
                    c_sin, c_cos = cell_sin[rows, :], cell_cos[rows, :]
                    hidden = []
                    for half in range(GROUP // 2):
                        cols = slice(half * two, (half + 1) * two)
                        value = c_sin * p_cos[:, cols] - c_cos * p_sin[:, cols]
                        hidden.append(value.astype(bf16))
                    y = matmul(jnp.concatenate(hidden, 1), spread_two[...]) + bias
                    bent = jnp.tanh(y * (LINEAR + CUBIC * (y * y)))
                    second[rows, inner * wide : (inner + 1) * wide] = (y + y * bent).astype(bf16)
                sums[rows, :] += matmul(second[rows, :], spread_three[...])

    own_q = sent_a.shape[3] // channels
    lane_z = lax.broadcasted_iota(jnp.int32, (NZ, LANES), 1) // channels
    lane_r = lax.broadcasted_iota(jnp.int32, (quarter, LANES), 1) // channels
    scale = 1.0 / math.sqrt(PB)

    def parcels(part):
        block, begin, some = parts[part]
        flat = jnp.zeros((NZ, LANES), f32)
        for slot in range(some):
            rows = slice(slot * NZ, (slot + 1) * NZ)
            total = sums[rows, 0:LANES] + sums[rows, LANES:]
            total = total + pltpu.roll(total, 2 * channels, 1)
            total = total + pltpu.roll(total, channels, 1)
            total = jnp.where(begin + slot < live_ref[block], total * scale, 0.0)
            flat = jnp.where(lane_z == slot, total, flat)
            tight = total[0:quarter]
            for at in range(1, GROUP):
                tight = jnp.where(lane_r == at, total[at * quarter : (at + 1) * quarter], tight)
            dense[begin + slot] = tight
        modes = matmul(z_table_ref[...], split_rows(flat))
        span = 2 * cols_y
        for slot in range(some):
            lanes = slice(slot * channels, (slot + 1) * channels)
            joined = jnp.concatenate(
                [modes[q * span : (q + 1) * span, lanes] for q in range(own_q)], 1
            )
            for half in range(2):
                sent_a[part, :, half * some + slot, :] = joined[
                    half * cols_y : (half + 1) * cols_y
                ]

    def raws(block):
        for dest in range(cols_y):
            chosen = jnp.zeros((quarter, LANES), f32)
            for slot in range(listed):
                chosen = jnp.where(owner_ref[block, slot] == dest, dense[slot], chosen)
            raw_sent[dest, block] = chosen

    def send(source, target, stage, x, y):
        pltpu.make_async_remote_copy(
            src_ref=source,
            dst_ref=target,
            send_sem=sends.at[stage],
            recv_sem=recvs.at[stage],
            device_id={"gx": x, "gy": y},
        ).start()

    def keep(source, target, stage):
        pltpu.make_async_copy(source, target, recvs.at[stage]).start()

    def spread(part):
        if part == len(parts) - 1:
            sent_b[...] = sent_a[part, :, 0 : sent_b.shape[1], :].astype(bf16)

            def last(x, y):
                send(sent_b.at[y], got_b.at[me], part, x, y)

            everyone(last)
            keep(sent_b.at[mine_y], got_b.at[me], part)
            return
        rows = pl.ds(0, 2 * parts[part][2])

        def go(x, y):
            send(sent_a.at[part, y, rows], got_a.at[part, me, rows], part, x, y)

        everyone(go)
        keep(sent_a.at[part, mine_y, rows], got_a.at[part, me, rows], part)

    def arrive(target, stage):
        pltpu.make_async_copy(target, target, recvs.at[stage]).wait()

    def depart(part, stage):
        pltpu.make_async_copy(part, part, sends.at[stage]).wait()

    stage_code = len(parts)
    stage_raw, stage_d = stage_code + 1, stage_code + 2
    stage_e = stage_d + sent_d.shape[0]

    for part, (block, begin, some) in enumerate(parts):
        if begin == 0:
            points(block)
        pairs(block, begin, some)
        parcels(part)
        if part == 0:
            pl.semaphore_wait(barrier, count - 1)

            def tell(x, y):
                send(code_sent, code_got.at[me], stage_code, x, y)

            everyone(tell)
            keep(code_sent, code_got.at[me], stage_code)
        spread(part)
        if begin + some == listed:
            raws(block)

    arrive(code_got, stage_code)
    own_p = sent_d.shape[0]
    modes = own_p * cols_x
    slots = modes * 2
    lanes_w = got_a.shape[3]

    def waves(turns):
        angle = (turns - jnp.floor(turns)) * (2.0 * math.pi)
        return jnp.cos(angle), jnp.sin(angle)

    starts = [0]
    for part, (block, begin, some) in enumerate(parts):
        each = 2 * some
        depth = count * each
        column = lax.broadcasted_iota(jnp.int32, (1, depth), 1)
        source = column // each
        row = lax.broadcasted_iota(jnp.int32, (slots, depth), 0)
        which = (row // 8) * 4 + row % 4
        freq_x = jnp.where(which < modes // 2, which, size_x - modes + which)
        part_out = (row // 4) % 2
        part_in = (column // some) % 2
        quarters = (part_out - part_in).astype(f32) * 0.25
        p_at = mine_x * own_p + lax.broadcasted_iota(jnp.int32, (own_p, depth), 0)
        freq_y = jnp.where(p_at < modes // 2, p_at, size_y - modes + p_at)
        owns = (
            lax.broadcasted_iota(jnp.int32, (count, depth), 1) // each
            == lax.broadcasted_iota(jnp.int32, (count, depth), 0)
        )
        codes = jnp.concatenate([code_got[:, part, :].astype(f32)] * (depth // LANES), 1)
        code = jnp.sum(jnp.where(owns, codes, 0.0), axis=0, keepdims=True).astype(jnp.int32)
        tile = code % (CX * CY)
        x_at = CX * (source // cols_y) + tile // CY
        y_at = CY * (code // (CX * CY)) + tile % CY
        x_cos, x_sin = waves((freq_x * x_at).astype(f32) * (1.0 / size_x) + quarters)
        y_cos, y_sin = waves((freq_y * y_at).astype(f32) * (1.0 / size_y))
        start = starts[part]
        for p in range(own_p):
            value = x_cos * y_cos[p : p + 1] - x_sin * y_sin[p : p + 1]
            high, low = halves(value)
            rows = slice(p * slots, (p + 1) * slots)
            kinds = [high, low] if part == len(parts) - 1 else [high, high, low]
            for index, kind in enumerate(kinds):
                phases[rows, start + index * depth : start + (index + 1) * depth] = kind
        starts.append(start + len(kinds) * depth)
    for part, (block, begin, some) in enumerate(parts[:-1]):
        rows = pl.ds(0, 2 * some)
        arrive(got_a.at[part, :, rows], part)
        splits[starts[part] : starts[part + 1], :] = split_rows(
            got_a[part, :, 0 : 2 * some].reshape(count * 2 * some, lanes_w)
        )
    seen = slice(0, starts[-2])
    spectra[...] = matmul(phases[:, seen], splits[seen, :])
    arrive(got_b, len(parts) - 1)
    value = got_b[...].astype(f32).reshape(-1, lanes_w).astype(bf16)
    splits[starts[-2] : starts[-1], :] = jnp.concatenate([value, value], 0)
    seen = slice(starts[-2], starts[-1])
    spectra[...] += matmul(phases[:, seen], splits[seen, :])

    for step in range(1, cols_y):
        other = near_y[step]
        send(raw_sent.at[other], held_ref.at[mine_y], stage_raw, mine_x, other)
    keep(raw_sent.at[mine_y], held_ref.at[mine_y], stage_raw)

    for load in loads:
        load.wait()
    quad = 8 * channels
    bands = LANES // channels
    row_of = lax.broadcasted_iota(jnp.int32, (8, LANES), 0)
    lane_of = lax.broadcasted_iota(jnp.int32, (8, LANES), 1)
    band = lane_of // channels
    own_four = [row_of % 4 == 2 * side + lane_of // (2 * channels) for side in range(2)]
    negate = row_of < 4
    fours = modes // 4
    tiles = max(1, lanes_w // LANES)
    width = lanes_w // tiles
    each = width // channels
    for p in range(own_p):
        for group in range(fours):
            rows = slice((p * fours + group) * 8, (p * fours + group) * 8 + 8)
            for at_tile in range(tiles):
                cols = slice(at_tile * width, (at_tile + 1) * width)
                plain = jnp.concatenate([spectra[rows, cols]] * (LANES // width), 1)
                turned = pltpu.roll(plain, 4, 0)
                turned = jnp.where(negate, -turned, turned)
                plains = [plain] + [pltpu.roll(plain, r * channels, 1) for r in range(1, bands)]
                turns = [turned] + [pltpu.roll(turned, r * channels, 1) for r in range(1, bands)]
                outs = []
                for q in range(each):
                    both = plains[-q % bands]
                    for at in range(1, bands):
                        kind = turns if at % 2 else plains
                        both = jnp.where(band == at, kind[(at - q) % bands], both)
                    both = jnp.concatenate([jnp.where(own, both, 0.0) for own in own_four], 1)
                    high, rest = halves(both)
                    tile = weights[group * 4 : group * 4 + 4, p, at_tile * each + q]
                    out = matmul(jnp.concatenate([high, rest], 0), tile.reshape(quad, channels))
                    outs.append(out[:8] + out[8:])
                mixed[group * 8 : group * 8 + 8, cols] = jnp.concatenate(outs, 1)
        along_x = matmul(backward_ref[...], split_rows(mixed[...]))
        sent_d[p] = along_x.reshape(sent_d.shape[1:])
        for step in range(1, cols_x):
            other = near_x[step]
            send(sent_d.at[p, other], got_d.at[p, mine_x], stage_d + p, other, mine_y)
        keep(sent_d.at[p, mine_x], got_d.at[p, mine_x], stage_d + p)
    for p in range(own_p - 1):
        arrive(got_d.at[p], stage_d + p)
        part = matmul(lift_ref[p], split_rows(got_d[p].reshape(-1, lanes_w)))
        lifted[...] = part if p == 0 else lifted[...] + part
    p = own_p - 1
    arrive(got_d.at[p], stage_d + p)
    for piece in range(tiles):
        cols = slice(piece * width, (piece + 1) * width)
        along_y = matmul(lift_ref[p], split_rows(got_d[p, :, :, cols].reshape(-1, width)))
        if p:
            along_y = lifted[:, cols] + along_y
        sent_e[piece] = along_y.reshape(sent_e.shape[1:])
        for step in range(1, cols_y):
            other = near_y[step]
            send(
                sent_e.at[piece, other],
                back_ref.at[piece, mine_y],
                stage_e + piece,
                mine_x,
                other,
            )
        keep(sent_e.at[piece, mine_y], back_ref.at[piece, mine_y], stage_e + piece)
    codes_ref[...] = code_got[pl.ds(mine_x * cols_y, cols_y)]
    for part, (block, begin, some) in enumerate(parts[:-1]):
        depart(got_a.at[part, pl.ds(0, count - 1), pl.ds(0, 2 * some)], part)
    depart(got_b.at[pl.ds(0, count - 1)], len(parts) - 1)
    depart(code_got.at[pl.ds(0, count - 1)], stage_code)
    depart(raw_sent.at[pl.ds(0, cols_y - 1)], stage_raw)
    for p in range(own_p):
        depart(sent_d.at[p, pl.ds(0, cols_x - 1)], stage_d + p)
    arrive(held_ref, stage_raw)
    for piece in range(tiles):
        arrive(back_ref.at[piece], stage_e + piece)
        depart(sent_e.at[piece, pl.ds(0, cols_y - 1)], stage_e + piece)


def encoder(
    features,
    offsets,
    point_cell,
    tile_owner,
    tile_local,
    live_count,
    w_first,
    b_first,
    w_second,
    b_second,
    w_third,
    w_modes,
    z_table,
    backward,
    lift,
):
    cols_x, cols_y = lax.axis_size("gx"), lax.axis_size("gy")
    count = cols_x * cols_y
    own_p, own_q = w_modes.shape[1:3]
    modes, channels = w_modes.shape[0], w_modes.shape[-1]
    hid = w_third.shape[1]
    blocks, listed = tile_owner.shape
    lanes = own_q * channels
    wide = GROUP * hid
    quarter = PB // GROUP
    depth = count * 2 * listed
    slots = modes * 2 * own_p
    smem = pl.BlockSpec(memory_space=pltpu.SMEM)
    vmem = pl.BlockSpec(memory_space=pltpu.VMEM)
    pieces = max(1, lanes // LANES)
    width = lanes // pieces
    anywhere = pl.BlockSpec(memory_space=pl.ANY)
    last = (pieces, cols_y, 2 * CX * CY, width)
    parcel = (own_p, cols_x, 2 * CX, lanes)
    number = len(parts_of(blocks, listed))
    stages = number + 2 + own_p + pieces
    return pl.pallas_call(
        encoder_kernel,
        out_shape=(
            jax.ShapeDtypeStruct((cols_y, 8, LANES), jnp.int32),
            jax.ShapeDtypeStruct((cols_y, blocks, quarter, LANES), f32),
            jax.ShapeDtypeStruct(last, f32),
        ),
        in_specs=[smem] * 3 + [vmem] * 9 + [anywhere] * 3,
        out_specs=(vmem, anywhere, anywhere),
        scratch_shapes=[
            pltpu.VMEM(w_modes.shape, w_modes.dtype),
            pltpu.VMEM(backward.shape, backward.dtype),
            pltpu.VMEM(lift.shape, lift.dtype),
            pltpu.VMEM((listed * NZ, 2 * hid), f32),
            pltpu.VMEM((listed * NZ, 2 * hid), f32),
            pltpu.VMEM((quarter, wide), f32),
            pltpu.VMEM((quarter, wide), f32),
            pltpu.VMEM((wide, wide), bf16),
            pltpu.VMEM((UNROLL * wide, 2 * GROUP * channels), bf16),
            pltpu.VMEM((quarter, GROUP * channels), f32),
            pltpu.VMEM((listed * NZ, UNROLL * wide), bf16),
            pltpu.VMEM((listed * NZ, 2 * GROUP * channels), f32),
            pltpu.VMEM((listed, quarter, LANES), f32),
            pltpu.VMEM((8, LANES), jnp.int32),
            pltpu.VMEM((count, 8, LANES), jnp.int32),
            pltpu.VMEM((number, cols_y, 2 * listed, lanes), f32),
            pltpu.VMEM((number, count, 2 * listed, lanes), f32),
            pltpu.VMEM((cols_y, 2 * (listed - listed // 2), lanes), bf16),
            pltpu.VMEM((count, 2 * (listed - listed // 2), lanes), bf16),
            pltpu.VMEM((cols_y, blocks, quarter, LANES), f32),
            pltpu.VMEM((slots, blocks * 3 * depth), bf16),
            pltpu.VMEM((blocks * 3 * depth, lanes), bf16),
            pltpu.VMEM((slots, lanes), f32),
            pltpu.VMEM((modes * 2, lanes), f32),
            pltpu.VMEM((lift.shape[1], lanes), f32),
            pltpu.VMEM(parcel, f32),
            pltpu.VMEM(parcel, f32),
            pltpu.VMEM(last, f32),
            pltpu.SemaphoreType.DMA((3,)),
            pltpu.SemaphoreType.DMA((stages,)),
            pltpu.SemaphoreType.DMA((stages,)),
        ],
        compiler_params=pltpu.CompilerParams(collective_id=0, has_side_effects=True),
        name="encoder",
    )(
        tile_owner,
        tile_local,
        live_count,
        features,
        offsets,
        point_cell[None],
        w_first.T,
        b_first[None],
        w_second,
        b_second[None],
        w_third,
        z_table,
        backward,
        lift,
        w_modes,
    )


def decoder_kernel(
    codes_ref,
    held_ref,
    back_hbm,
    inverse_ref,
    w_point_ref,
    b_point_ref,
    out_ref,
    back_ref,
    rolled,
    before,
    done,
    out_sem,
    back_sem,
):
    load = pltpu.make_async_copy(back_hbm, back_ref, back_sem)
    load.start()
    cols_y, blocks, quarter = held_ref.shape[:3]
    channels = w_point_ref.shape[0]
    mine_y = lax.axis_index("gy")
    codes_at = len(parts_of(blocks, GROUP))
    groups = LANES // channels
    pieces, width = back_ref.shape[0], back_ref.shape[3]
    each = width // channels
    bias = jnp.concatenate([b_point_ref[...]] * channels, 0).T[:, 0:1]
    before[...] = jnp.zeros_like(before)
    turned = w_point_ref[...].astype(f32).T.astype(bf16)
    turned = jnp.concatenate([turned, turned], 1)
    items = []
    for source in range(cols_y):
        for block in range(blocks):
            flipped = held_ref[source, block].T
            items.append(
                jnp.concatenate(
                    [flipped[j * channels : (j + 1) * channels] for j in range(groups)], 1
                )
            )
    high, low = halves(jnp.concatenate(items, 1))
    points = matmul(turned, jnp.concatenate([high, low], 0))
    for source in range(cols_y):
        for block in range(blocks):
            tile = codes_ref[source, codes_at + block, mine_y]
            item = source * blocks + block

            @pl.when(tile >= 0)
            def _():
                before[tile] += points[:, item * NZ : (item + 1) * NZ]

    load.wait()
    for piece in range(pieces):
        value = back_ref[piece].reshape(cols_y * 2 * CX * CY, width)
        value = jnp.concatenate([value] * (LANES // width), 1)
        for shift in range(groups):
            rolled[piece, shift] = pltpu.roll(value, shift * channels, 1) if shift else value
    spans = 2 * cols_y
    lane = lax.broadcasted_iota(jnp.int32, (spans, LANES), 1) // channels
    root = math.sqrt(2.0 / math.pi)
    moves = []
    for chunk in range(CX * CY // groups):
        rows = []
        for q in range(pieces * each):
            found = jnp.zeros((spans, LANES), f32)
            for j in range(groups):
                piece = rolled[
                    q // each,
                    (j - q % each) % groups,
                    pl.ds(chunk * groups + j, spans, stride=CX * CY),
                    :,
                ]
                found = jnp.where(lane == j, piece, found)
            rows.append(found)
        spectral = lax.dot_general(
            split_rows(jnp.concatenate(rows, 0)),
            inverse_ref[...],
            (((0,), (0,)), ((), ())),
            preferred_element_type=f32,
        )
        for j in range(groups):
            tile = chunk * groups + j
            x = spectral[j * channels : (j + 1) * channels] + (before[tile] + bias)
            half = 0.5 * x
            bent = jnp.tanh(x * (root + (0.044715 * root) * (x * x)))
            done[tile // CY, tile % CY] = half + half * bent
        at = (chunk * groups // CY, pl.ds(chunk * groups % CY, groups))
        move = pltpu.make_async_copy(done.at[at], out_ref.at[at], out_sem.at[chunk])
        move.start()
        moves.append(move)
    for move in moves:
        move.wait()


def decoder(codes, held, back, inverse, w_point, b_point):
    smem = pl.BlockSpec(memory_space=pltpu.SMEM)
    vmem = pl.BlockSpec(memory_space=pltpu.VMEM)
    channels = w_point.shape[0]
    rows = back.shape[1] * back.shape[2]
    shape = (CX, CY, channels, NZ)
    return pl.pallas_call(
        decoder_kernel,
        out_shape=jax.ShapeDtypeStruct(shape, f32),
        in_specs=[smem, vmem, pl.BlockSpec(memory_space=pl.ANY)] + [vmem] * 3,
        out_specs=pl.BlockSpec(memory_space=pl.ANY),
        scratch_shapes=[
            pltpu.VMEM(back.shape, f32),
            pltpu.VMEM((back.shape[0], LANES // channels, rows, LANES), f32),
            pltpu.VMEM((CX * CY, channels, NZ), f32),
            pltpu.VMEM(shape, f32),
            pltpu.SemaphoreType.DMA((CX * CY * channels // LANES,)),
            pltpu.SemaphoreType.DMA,
        ],
        name="decoder",
    )(codes, held, back, inverse, w_point, b_point[None])


def local(
    features,
    offsets,
    point_cell,
    tile_owner,
    tile_local,
    live_count,
    w_first,
    b_first,
    w_second,
    b_second,
    w_third,
    w_point,
    b_point,
    w_modes,
):
    z_table, backward, lift, inverse = tables(
        lax.axis_size("gx"), lax.axis_size("gy"), w_modes.shape[0]
    )
    codes, held, back = encoder(
        features,
        offsets,
        point_cell,
        tile_owner,
        tile_local,
        live_count,
        w_first,
        b_first,
        w_second,
        b_second,
        w_third,
        w_modes,
        z_table,
        backward,
        lift,
    )
    return decoder(codes, held, back, inverse, w_point, b_point)


def solution(mesh):
    placed = (
        P(None, ("gx", "gy")),
        P(None, ("gx", "gy")),
        P(("gx", "gy")),
        P(("gx", "gy"), None),
        P(("gx", "gy"), None),
        P(("gx", "gy")),
        P(),
        P(),
        P(),
        P(),
        P(),
        P(),
        P(),
        P(None, "gx", "gy", None, None, None),
    )
    return jax.shard_map(
        local, mesh=mesh, in_specs=placed, out_specs=P("gx", "gy", None, None), check_vma=False
    )
```

```python
import math

import jax
import numpy as np
import jax.numpy as jnp
from jax import lax
from jax.experimental import pallas as pl
from jax.experimental.pallas import tpu as pltpu
from jax.sharding import PartitionSpec as P

NZ = 128
CX = 4
CY = 8
SPAN = 16
PB = 128
LANES = 128

GROUP = 4
UNROLL = 16

LINEAR = 2.0 * math.sqrt(2.0 / math.pi)
CUBIC = 4.0 * 0.044715 * LINEAR

f32 = jnp.float32
bf16 = jnp.bfloat16


def halves(value):
    high = value.astype(bf16)
    return high, (value - high.astype(f32)).astype(bf16)


def split_rows(value):
    high, low = halves(value)
    return jnp.concatenate([high, low, high], 0)


def split_table(table):
    table = np.asarray(table, np.float32)
    high = table.astype(jnp.bfloat16)
    low = (table - high.astype(np.float32)).astype(jnp.bfloat16)
    return np.concatenate([high, high, low], 1)


def matmul(left, right):
    return jnp.dot(left, right, preferred_element_type=f32)


def tables(cols_x, cols_y, modes):
    size_x, size_y = CX * cols_x, CY * cols_y
    own_p, own_q = modes // cols_x, modes // cols_y
    scale = 1.0 / math.sqrt(size_x * size_y * NZ)

    def frequencies(length):
        order = np.arange(modes)
        return np.where(order < modes // 2, order, length - modes + order)

    def turn(angle):
        cosine, sine = np.cos(angle), np.sin(angle)
        return np.array([[cosine, -sine], [sine, cosine]])

    z_turns = 2 * np.pi * (np.outer(np.arange(modes), np.arange(NZ)) % NZ) / NZ
    waves = np.stack([np.cos(z_turns), -np.sin(z_turns)], 0) * scale
    waves = waves.reshape(2, cols_y, own_q, NZ)
    z_table = waves.transpose(2, 0, 1, 3).reshape(-1, NZ)
    inverse = waves.transpose(2, 1, 0, 3).reshape(-1, NZ)
    inverse = np.asarray(inverse, np.float32)
    high = inverse.astype(jnp.bfloat16)
    low = (inverse - high.astype(np.float32)).astype(jnp.bfloat16)
    inverse = np.concatenate([high, high, low], 0)
    x_turns = 2 * np.pi * (np.outer(frequencies(size_x), np.arange(size_x)) % size_x) / size_x
    backward = turn(x_turns).reshape(2, 2, modes // 4, 4, cols_x, CX)
    backward = np.einsum("srgkdx->dsxgrk", backward).reshape(-1, modes * 2)
    y_turns = 2 * np.pi * (np.outer(frequencies(size_y), np.arange(size_y)) % size_y) / size_y
    lift = turn(y_turns).reshape(2, 2, cols_x, own_p, cols_y, CY)
    lift = np.einsum("srepdy,xX->pdsxyerX", lift, np.eye(CX))
    lift = lift.reshape(own_p, 2 * CX * size_y, -1)
    lift = np.stack([split_table(each) for each in lift], 0)
    return split_table(z_table), split_table(backward), lift, inverse


def parts_of(blocks, listed):
    whole = [(block, 0, listed) for block in range(blocks - 1)]
    half = listed // 2
    return whole + [(blocks - 1, 0, half), (blocks - 1, half, listed - half)]


def encoder_kernel(
    owner_ref,
    local_ref,
    live_ref,
    features_ref,
    offsets_ref,
    cells_ref,
    turned_first_ref,
    b_first_ref,
    w_second_ref,
    b_second_ref,
    w_third_ref,
    z_table_ref,
    backward_hbm,
    lift_hbm,
    modes_ref,
    codes_ref,
    held_ref,
    back_ref,
    weights,
    backward_ref,
    lift_ref,
    cell_sin,
    cell_cos,
    point_sin,
    point_cos,
    spread_two,
    spread_three,
    feats,
    second,
    sums,
    dense,
    code_sent,
    code_got,
    sent_a,
    got_a,
    sent_b,
    got_b,
    raw_sent,
    phases,
    splits,
    spectra,
    mixed,
    lifted,
    sent_d,
    got_d,
    sent_e,
    load_sem,
    sends,
    recvs,
):
    cols_x, cols_y = lax.axis_size("gx"), lax.axis_size("gy")
    mine_x, mine_y = lax.axis_index("gx"), lax.axis_index("gy")
    count = cols_x * cols_y
    me = mine_x * cols_y + mine_y
    blocks, listed = owner_ref.shape
    hid = w_second_ref.shape[0]
    channels = w_third_ref.shape[0]
    wide = GROUP * hid
    two = 2 * hid
    quarter = PB // GROUP
    size_x, size_y = CX * cols_x, CY * cols_y
    loads = []
    for index, (source, target) in enumerate(
        ((modes_ref, weights), (backward_hbm, backward_ref), (lift_hbm, lift_ref))
    ):
        load = pltpu.make_async_copy(source, target, load_sem.at[index])
        load.start()
        loads.append(load)

    def around(mine, step, size):
        other = mine + step
        return jnp.where(other >= size, other - size, other)

    near_x = [around(mine_x, step, cols_x) for step in range(cols_x)]
    near_y = [around(mine_y, step, cols_y) for step in range(cols_y)]

    def everyone(body):
        if count <= 32:
            for x in near_x:
                for y in near_y:
                    if x is not near_x[0] or y is not near_y[0]:
                        body(x, y)
        else:

            @pl.loop(1, count)
            def _(step):
                other = lax.rem(me + step, count)
                x = lax.div(other, cols_y)
                body(x, other - x * cols_y)

    barrier = pltpu.get_barrier_semaphore()

    def greet(x, y):
        pl.semaphore_signal(barrier, inc=1, device_id={"gx": x, "gy": y})

    everyone(greet)

    turned_two = (w_second_ref[...].astype(f32).T * 0.5).astype(bf16)
    turned_three = w_third_ref[...].astype(f32).T
    spread_two[...] = jnp.zeros_like(spread_two)
    spread_three[...] = jnp.zeros_like(spread_three)
    for part in range(GROUP):
        rows = slice(part * hid, (part + 1) * hid)
        spread_two[rows, rows] = turned_two
    bias = jnp.concatenate([b_second_ref[...] * 0.5] * GROUP, 1)
    wide_three = jnp.concatenate([turned_three] * GROUP, 1)
    coarse_y, coarse_z = size_y // SPAN, NZ // SPAN
    cells = cells_ref[...]
    coarse = jnp.concatenate(
        [cells // (coarse_y * coarse_z), cells // coarse_z % coarse_y, cells % coarse_z], 0
    )
    places = coarse.astype(f32) * SPAN + offsets_ref[...].astype(f32)
    places = jnp.concatenate([places, jnp.zeros((5, places.shape[1]), f32)], 0)
    turned_first = turned_first_ref[...].astype(f32)
    double_first = jnp.concatenate([turned_first, turned_first], 1)
    features = features_ref[...].astype(f32)

    steps = lax.broadcasted_iota(jnp.int32, (24, two), 0)
    steps = jnp.where(steps < 16, steps * 8, steps - 16).astype(f32)
    steps = steps * double_first[2:3]
    cosine, sine = jnp.cos(steps), jnp.sin(steps)
    cos_fine, sin_fine = cosine[16:24], sine[16:24]
    bases = []
    for block in range(blocks):
        for slot in range(listed):
            tile = local_ref[block, slot]
            cell_x = (CX * mine_x + tile // CY).astype(f32)
            cell_y = (CY * owner_ref[block, slot] + tile % CY).astype(f32)
            bases.append(
                turned_first[0:1] * cell_x + turned_first[1:2] * cell_y + b_first_ref[...]
            )
    base = jnp.concatenate(bases, 0)
    base = jnp.concatenate([base, base], 1)
    base_sin, base_cos = jnp.sin(base), jnp.cos(base)
    code_lane = lax.broadcasted_iota(jnp.int32, (1, LANES), 1)
    code_rows = []
    parts = parts_of(blocks, listed)
    for block, begin, some in parts:
        row = jnp.zeros((1, LANES), jnp.int32)
        for slot in range(some):
            code = (
                owner_ref[block, begin + slot] * (CX * CY) + local_ref[block, begin + slot]
            )
            row = jnp.where(code_lane % some == slot, code, row)
        code_rows.append(row)
    for block in range(blocks):
        row = jnp.full((1, LANES), -1, jnp.int32)
        for slot in range(listed):
            alive = jnp.where(slot < live_ref[block], local_ref[block, slot], -1)
            row = jnp.where(code_lane == owner_ref[block, slot], alive, row)
        code_rows.append(row)
    code_rows.append(jnp.zeros((8 - len(code_rows), LANES), jnp.int32))
    code_sent[...] = jnp.concatenate(code_rows, 0)

    lane = lax.broadcasted_iota(jnp.int32, (quarter, two), 1)

    def points(block):
        here = slice(block * PB, (block + 1) * PB)
        spots = places[:, here].T
        for half in range(GROUP // 2):
            low = slice(2 * half * quarter, (2 * half + 1) * quarter)
            up = slice((2 * half + 1) * quarter, (2 * half + 2) * quarter)
            cols = slice(half * two, (half + 1) * two)
            side = 0.0
            for axis in range(3):
                spot = jnp.where(lane < hid, spots[low, axis : axis + 1], spots[up, axis : axis + 1])
                side = side + double_first[axis : axis + 1] * spot
            point_cos[:, cols] = jnp.cos(side)
            point_sin[:, cols] = jnp.sin(side)
        turned = features[:, here].T
        feats[...] = jnp.concatenate(
            [turned[j * quarter : (j + 1) * quarter] for j in range(GROUP)], 1
        )

    def pairs(block, begin, some):
        for slot in range(some):
            item = block * listed + begin + slot
            b_sin, b_cos = base_sin[item : item + 1], base_cos[item : item + 1]
            near_sin = sin_fine * b_cos + cos_fine * b_sin
            near_cos = cos_fine * b_cos - sin_fine * b_sin
            for step in range(NZ // 8):
                rows = slice(slot * NZ + step * 8, slot * NZ + step * 8 + 8)
                far_cos, far_sin = cosine[step : step + 1], sine[step : step + 1]
                cell_sin[rows, :] = far_cos * near_sin + far_sin * near_cos
                cell_cos[rows, :] = far_cos * near_cos - far_sin * near_sin
        sums[...] = jnp.zeros_like(sums)

        @pl.loop(0, quarter // UNROLL)
        def _(step):
            for inner in range(UNROLL):
                weigh = wide_three * feats[pl.ds(step * UNROLL + inner, 1), :]
                high, rest = halves(weigh)
                for part in range(GROUP):
                    rows = slice(inner * wide + part * hid, inner * wide + (part + 1) * hid)
                    cols = slice(part * channels, (part + 1) * channels)
                    spread_three[rows, part * channels : (part + 1) * channels] = high[:, cols]
                    spread_three[
                        rows, LANES + part * channels : LANES + (part + 1) * channels
                    ] = rest[:, cols]
            for slot in range(some):
                rows = slice(slot * NZ, (slot + 1) * NZ)
                for inner in range(UNROLL):
                    group = step * UNROLL + inner
                    p_cos, p_sin = point_cos[pl.ds(group, 1), :], point_sin[pl.ds(group, 1), :]
                    c_sin, c_cos = cell_sin[rows, :], cell_cos[rows, :]
                    hidden = []
                    for half in range(GROUP // 2):
                        cols = slice(half * two, (half + 1) * two)
                        value = c_sin * p_cos[:, cols] - c_cos * p_sin[:, cols]
                        hidden.append(value.astype(bf16))
                    y = matmul(jnp.concatenate(hidden, 1), spread_two[...]) + bias
                    bent = jnp.tanh(y * (LINEAR + CUBIC * (y * y)))
                    second[rows, inner * wide : (inner + 1) * wide] = (y + y * bent).astype(bf16)
                sums[rows, :] += matmul(second[rows, :], spread_three[...])

    own_q = sent_a.shape[3] // channels
    lane_z = lax.broadcasted_iota(jnp.int32, (NZ, LANES), 1) // channels
    lane_r = lax.broadcasted_iota(jnp.int32, (quarter, LANES), 1) // channels
    scale = 1.0 / math.sqrt(PB)

    def parcels(part):
        block, begin, some = parts[part]
        flat = jnp.zeros((NZ, LANES), f32)
        for slot in range(some):
            rows = slice(slot * NZ, (slot + 1) * NZ)
            total = sums[rows, 0:LANES] + sums[rows, LANES:]
            total = total + pltpu.roll(total, 2 * channels, 1)
            total = total + pltpu.roll(total, channels, 1)
            total = jnp.where(begin + slot < live_ref[block], total * scale, 0.0)
            flat = jnp.where(lane_z == slot, total, flat)
            tight = total[0:quarter]
            for at in range(1, GROUP):
                tight = jnp.where(lane_r == at, total[at * quarter : (at + 1) * quarter], tight)
            dense[begin + slot] = tight
        modes = matmul(z_table_ref[...], split_rows(flat))
        span = 2 * cols_y
        for slot in range(some):
            lanes = slice(slot * channels, (slot + 1) * channels)
            joined = jnp.concatenate(
                [modes[q * span : (q + 1) * span, lanes] for q in range(own_q)], 1
            )
            for half in range(2):
                sent_a[part, :, half * some + slot, :] = joined[
                    half * cols_y : (half + 1) * cols_y
                ]

    def raws(block):
        for dest in range(cols_y):
            chosen = jnp.zeros((quarter, LANES), f32)
            for slot in range(listed):
                chosen = jnp.where(owner_ref[block, slot] == dest, dense[slot], chosen)
            raw_sent[dest, block] = chosen

    def send(source, target, stage, x, y):
        pltpu.make_async_remote_copy(
            src_ref=source,
            dst_ref=target,
            send_sem=sends.at[stage],
            recv_sem=recvs.at[stage],
            device_id={"gx": x, "gy": y},
        ).start()

    def keep(source, target, stage):
        pltpu.make_async_copy(source, target, recvs.at[stage]).start()

    def spread(part):
        if part == len(parts) - 1:
            sent_b[...] = sent_a[part, :, 0 : sent_b.shape[1], :].astype(bf16)

            def last(x, y):
                send(sent_b.at[y], got_b.at[me], part, x, y)

            everyone(last)
            keep(sent_b.at[mine_y], got_b.at[me], part)
            return
        rows = pl.ds(0, 2 * parts[part][2])

        def go(x, y):
            send(sent_a.at[part, y, rows], got_a.at[part, me, rows], part, x, y)

        everyone(go)
        keep(sent_a.at[part, mine_y, rows], got_a.at[part, me, rows], part)

    def arrive(target, stage):
        pltpu.make_async_copy(target, target, recvs.at[stage]).wait()

    def depart(part, stage):
        pltpu.make_async_copy(part, part, sends.at[stage]).wait()

    stage_code = len(parts)
    stage_raw, stage_d = stage_code + 1, stage_code + 2
    stage_e = stage_d + sent_d.shape[0]

    for part, (block, begin, some) in enumerate(parts):
        if begin == 0:
            points(block)
        pairs(block, begin, some)
        parcels(part)
        if part == 0:
            pl.semaphore_wait(barrier, count - 1)

            def tell(x, y):
                send(code_sent, code_got.at[me], stage_code, x, y)

            everyone(tell)
            keep(code_sent, code_got.at[me], stage_code)
        spread(part)
        if begin + some == listed:
            raws(block)

    arrive(code_got, stage_code)
    own_p = sent_d.shape[0]
    modes = own_p * cols_x
    slots = modes * 2
    lanes_w = got_a.shape[3]

    def waves(turns):
        angle = (turns - jnp.floor(turns)) * (2.0 * math.pi)
        return jnp.cos(angle), jnp.sin(angle)

    starts = [0]
    for part, (block, begin, some) in enumerate(parts):
        each = 2 * some
        depth = count * each
        column = lax.broadcasted_iota(jnp.int32, (1, depth), 1)
        source = column // each
        row = lax.broadcasted_iota(jnp.int32, (slots, depth), 0)
        which = (row // 8) * 4 + row % 4
        freq_x = jnp.where(which < modes // 2, which, size_x - modes + which)
        part_out = (row // 4) % 2
        part_in = (column // some) % 2
        quarters = (part_out - part_in).astype(f32) * 0.25
        p_at = mine_x * own_p + lax.broadcasted_iota(jnp.int32, (own_p, depth), 0)
        freq_y = jnp.where(p_at < modes // 2, p_at, size_y - modes + p_at)
        owns = (
            lax.broadcasted_iota(jnp.int32, (count, depth), 1) // each
            == lax.broadcasted_iota(jnp.int32, (count, depth), 0)
        )
        codes = jnp.concatenate([code_got[:, part, :].astype(f32)] * (depth // LANES), 1)
        code = jnp.sum(jnp.where(owns, codes, 0.0), axis=0, keepdims=True).astype(jnp.int32)
        tile = code % (CX * CY)
        x_at = CX * (source // cols_y) + tile // CY
        y_at = CY * (code // (CX * CY)) + tile % CY
        x_cos, x_sin = waves((freq_x * x_at).astype(f32) * (1.0 / size_x) + quarters)
        y_cos, y_sin = waves((freq_y * y_at).astype(f32) * (1.0 / size_y))
        start = starts[part]
        for p in range(own_p):
            value = x_cos * y_cos[p : p + 1] - x_sin * y_sin[p : p + 1]
            high, low = halves(value)
            rows = slice(p * slots, (p + 1) * slots)
            kinds = [high, low] if part == len(parts) - 1 else [high, high, low]
            for index, kind in enumerate(kinds):
                phases[rows, start + index * depth : start + (index + 1) * depth] = kind
        starts.append(start + len(kinds) * depth)
    for part, (block, begin, some) in enumerate(parts[:-1]):
        rows = pl.ds(0, 2 * some)
        arrive(got_a.at[part, :, rows], part)
        splits[starts[part] : starts[part + 1], :] = split_rows(
            got_a[part, :, 0 : 2 * some].reshape(count * 2 * some, lanes_w)
        )
    seen = slice(0, starts[-2])
    spectra[...] = matmul(phases[:, seen], splits[seen, :])
    arrive(got_b, len(parts) - 1)
    value = got_b[...].astype(f32).reshape(-1, lanes_w).astype(bf16)
    splits[starts[-2] : starts[-1], :] = jnp.concatenate([value, value], 0)
    seen = slice(starts[-2], starts[-1])
    spectra[...] += matmul(phases[:, seen], splits[seen, :])

    for step in range(1, cols_y):
        other = near_y[step]
        send(raw_sent.at[other], held_ref.at[mine_y], stage_raw, mine_x, other)
    keep(raw_sent.at[mine_y], held_ref.at[mine_y], stage_raw)

    for load in loads:
        load.wait()
    quad = 8 * channels
    bands = LANES // channels
    row_of = lax.broadcasted_iota(jnp.int32, (8, LANES), 0)
    lane_of = lax.broadcasted_iota(jnp.int32, (8, LANES), 1)
    band = lane_of // channels
    own_four = [row_of % 4 == 2 * side + lane_of // (2 * channels) for side in range(2)]
    negate = row_of < 4
    fours = modes // 4
    tiles = max(1, lanes_w // LANES)
    width = lanes_w // tiles
    each = width // channels
    @pl.loop(0, own_p)
    def _(p):
        for group in range(fours):
            rows = pl.ds(pl.multiple_of((p * fours + group) * 8, 8), 8)
            for at_tile in range(tiles):
                cols = slice(at_tile * width, (at_tile + 1) * width)
                plain = jnp.concatenate([spectra[rows, cols]] * (LANES // width), 1)
                turned = pltpu.roll(plain, 4, 0)
                turned = jnp.where(negate, -turned, turned)
                plains = [plain] + [pltpu.roll(plain, r * channels, 1) for r in range(1, bands)]
                turns = [turned] + [pltpu.roll(turned, r * channels, 1) for r in range(1, bands)]
                outs = []
                for q in range(each):
                    both = plains[-q % bands]
                    for at in range(1, bands):
                        kind = turns if at % 2 else plains
                        both = jnp.where(band == at, kind[(at - q) % bands], both)
                    both = jnp.concatenate([jnp.where(own, both, 0.0) for own in own_four], 1)
                    high, rest = halves(both)
                    tile = weights[group * 4 : group * 4 + 4, p, at_tile * each + q]
                    out = matmul(jnp.concatenate([high, rest], 0), tile.reshape(quad, channels))
                    outs.append(out[:8] + out[8:])
                mixed[group * 8 : group * 8 + 8, cols] = jnp.concatenate(outs, 1)
        along_x = matmul(backward_ref[...], split_rows(mixed[...]))
        sent_d[p] = along_x.reshape(sent_d.shape[1:])
        for step in range(1, cols_x):
            other = near_x[step]
            send(sent_d.at[p, other], got_d.at[p, mine_x], stage_d + p, other, mine_y)
        keep(sent_d.at[p, mine_x], got_d.at[p, mine_x], stage_d + p)

    for p in range(own_p - 1):
        arrive(got_d.at[p], stage_d + p)
        part = matmul(lift_ref[p], split_rows(got_d[p].reshape(-1, lanes_w)))
        lifted[...] = part if p == 0 else lifted[...] + part
    p = own_p - 1
    arrive(got_d.at[p], stage_d + p)
    for piece in range(tiles):
        cols = slice(piece * width, (piece + 1) * width)
        along_y = matmul(lift_ref[p], split_rows(got_d[p, :, :, cols].reshape(-1, width)))
        if p:
            along_y = lifted[:, cols] + along_y
        sent_e[piece] = along_y.reshape(sent_e.shape[1:])
        for step in range(1, cols_y):
            other = near_y[step]
            send(
                sent_e.at[piece, other],
                back_ref.at[piece, mine_y],
                stage_e + piece,
                mine_x,
                other,
            )
        keep(sent_e.at[piece, mine_y], back_ref.at[piece, mine_y], stage_e + piece)
    codes_ref[...] = code_got[pl.ds(mine_x * cols_y, cols_y)]
    for part, (block, begin, some) in enumerate(parts[:-1]):
        depart(got_a.at[part, pl.ds(0, count - 1), pl.ds(0, 2 * some)], part)
    depart(got_b.at[pl.ds(0, count - 1)], len(parts) - 1)
    depart(code_got.at[pl.ds(0, count - 1)], stage_code)
    depart(raw_sent.at[pl.ds(0, cols_y - 1)], stage_raw)
    for p in range(own_p):
        depart(sent_d.at[p, pl.ds(0, cols_x - 1)], stage_d + p)
    arrive(held_ref, stage_raw)
    for piece in range(tiles):
        arrive(back_ref.at[piece], stage_e + piece)
        depart(sent_e.at[piece, pl.ds(0, cols_y - 1)], stage_e + piece)


def encoder(
    features,
    offsets,
    point_cell,
    tile_owner,
    tile_local,
    live_count,
    w_first,
    b_first,
    w_second,
    b_second,
    w_third,
    w_modes,
    z_table,
    backward,
    lift,
):
    cols_x, cols_y = lax.axis_size("gx"), lax.axis_size("gy")
    count = cols_x * cols_y
    own_p, own_q = w_modes.shape[1:3]
    modes, channels = w_modes.shape[0], w_modes.shape[-1]
    hid = w_third.shape[1]
    blocks, listed = tile_owner.shape
    lanes = own_q * channels
    wide = GROUP * hid
    quarter = PB // GROUP
    depth = count * 2 * listed
    slots = modes * 2 * own_p
    smem = pl.BlockSpec(memory_space=pltpu.SMEM)
    vmem = pl.BlockSpec(memory_space=pltpu.VMEM)
    pieces = max(1, lanes // LANES)
    width = lanes // pieces
    anywhere = pl.BlockSpec(memory_space=pl.ANY)
    last = (pieces, cols_y, 2 * CX * CY, width)
    parcel = (own_p, cols_x, 2 * CX, lanes)
    number = len(parts_of(blocks, listed))
    stages = number + 2 + own_p + pieces
    return pl.pallas_call(
        encoder_kernel,
        out_shape=(
            jax.ShapeDtypeStruct((cols_y, 8, LANES), jnp.int32),
            jax.ShapeDtypeStruct((cols_y, blocks, quarter, LANES), f32),
            jax.ShapeDtypeStruct(last, f32),
        ),
        in_specs=[smem] * 3 + [vmem] * 9 + [anywhere] * 3,
        out_specs=(vmem, anywhere, anywhere),
        scratch_shapes=[
            pltpu.VMEM(w_modes.shape, w_modes.dtype),
            pltpu.VMEM(backward.shape, backward.dtype),
            pltpu.VMEM(lift.shape, lift.dtype),
            pltpu.VMEM((listed * NZ, 2 * hid), f32),
            pltpu.VMEM((listed * NZ, 2 * hid), f32),
            pltpu.VMEM((quarter, wide), f32),
            pltpu.VMEM((quarter, wide), f32),
            pltpu.VMEM((wide, wide), bf16),
            pltpu.VMEM((UNROLL * wide, 2 * GROUP * channels), bf16),
            pltpu.VMEM((quarter, GROUP * channels), f32),
            pltpu.VMEM((listed * NZ, UNROLL * wide), bf16),
            pltpu.VMEM((listed * NZ, 2 * GROUP * channels), f32),
            pltpu.VMEM((listed, quarter, LANES), f32),
            pltpu.VMEM((8, LANES), jnp.int32),
            pltpu.VMEM((count, 8, LANES), jnp.int32),
            pltpu.VMEM((number, cols_y, 2 * listed, lanes), f32),
            pltpu.VMEM((number, count, 2 * listed, lanes), f32),
            pltpu.VMEM((cols_y, 2 * (listed - listed // 2), lanes), bf16),
            pltpu.VMEM((count, 2 * (listed - listed // 2), lanes), bf16),
            pltpu.VMEM((cols_y, blocks, quarter, LANES), f32),
            pltpu.VMEM((slots, blocks * 3 * depth), bf16),
            pltpu.VMEM((blocks * 3 * depth, lanes), bf16),
            pltpu.VMEM((slots, lanes), f32),
            pltpu.VMEM((modes * 2, lanes), f32),
            pltpu.VMEM((lift.shape[1], lanes), f32),
            pltpu.VMEM(parcel, f32),
            pltpu.VMEM(parcel, f32),
            pltpu.VMEM(last, f32),
            pltpu.SemaphoreType.DMA((3,)),
            pltpu.SemaphoreType.DMA((stages,)),
            pltpu.SemaphoreType.DMA((stages,)),
        ],
        compiler_params=pltpu.CompilerParams(collective_id=0, has_side_effects=True),
        name="encoder",
    )(
        tile_owner,
        tile_local,
        live_count,
        features,
        offsets,
        point_cell[None],
        w_first.T,
        b_first[None],
        w_second,
        b_second[None],
        w_third,
        z_table,
        backward,
        lift,
        w_modes,
    )


def decoder_kernel(
    codes_ref,
    held_ref,
    back_hbm,
    inverse_ref,
    w_point_ref,
    b_point_ref,
    out_ref,
    back_ref,
    rolled,
    before,
    done,
    out_sem,
    back_sem,
):
    load = pltpu.make_async_copy(back_hbm, back_ref, back_sem)
    load.start()
    cols_y, blocks, quarter = held_ref.shape[:3]
    channels = w_point_ref.shape[0]
    mine_y = lax.axis_index("gy")
    codes_at = len(parts_of(blocks, GROUP))
    groups = LANES // channels
    pieces, width = back_ref.shape[0], back_ref.shape[3]
    each = width // channels
    bias = jnp.concatenate([b_point_ref[...]] * channels, 0).T[:, 0:1]
    before[...] = jnp.zeros_like(before)
    turned = w_point_ref[...].astype(f32).T.astype(bf16)
    turned = jnp.concatenate([turned, turned], 1)
    items = []
    for source in range(cols_y):
        for block in range(blocks):
            flipped = held_ref[source, block].T
            items.append(
                jnp.concatenate(
                    [flipped[j * channels : (j + 1) * channels] for j in range(groups)], 1
                )
            )
    high, low = halves(jnp.concatenate(items, 1))
    points = matmul(turned, jnp.concatenate([high, low], 0))
    for source in range(cols_y):
        for block in range(blocks):
            tile = codes_ref[source, codes_at + block, mine_y]
            item = source * blocks + block

            @pl.when(tile >= 0)
            def _():
                before[tile] += points[:, item * NZ : (item + 1) * NZ]

    load.wait()
    for piece in range(pieces):
        value = back_ref[piece].reshape(cols_y * 2 * CX * CY, width)
        value = jnp.concatenate([value] * (LANES // width), 1)
        for shift in range(groups):
            rolled[piece, shift] = pltpu.roll(value, shift * channels, 1) if shift else value
    spans = 2 * cols_y
    lane = lax.broadcasted_iota(jnp.int32, (spans, LANES), 1) // channels
    root = math.sqrt(2.0 / math.pi)
    moves = []
    for chunk in range(CX * CY // groups):
        rows = []
        for q in range(pieces * each):
            found = jnp.zeros((spans, LANES), f32)
            for j in range(groups):
                piece = rolled[
                    q // each,
                    (j - q % each) % groups,
                    pl.ds(chunk * groups + j, spans, stride=CX * CY),
                    :,
                ]
                found = jnp.where(lane == j, piece, found)
            rows.append(found)
        spectral = lax.dot_general(
            split_rows(jnp.concatenate(rows, 0)),
            inverse_ref[...],
            (((0,), (0,)), ((), ())),
            preferred_element_type=f32,
        )
        for j in range(groups):
            tile = chunk * groups + j
            x = spectral[j * channels : (j + 1) * channels] + (before[tile] + bias)
            half = 0.5 * x
            bent = jnp.tanh(x * (root + (0.044715 * root) * (x * x)))
            done[tile // CY, tile % CY] = half + half * bent
        at = (chunk * groups // CY, pl.ds(chunk * groups % CY, groups))
        move = pltpu.make_async_copy(done.at[at], out_ref.at[at], out_sem.at[chunk])
        move.start()
        moves.append(move)
    for move in moves:
        move.wait()


def decoder(codes, held, back, inverse, w_point, b_point):
    smem = pl.BlockSpec(memory_space=pltpu.SMEM)
    vmem = pl.BlockSpec(memory_space=pltpu.VMEM)
    channels = w_point.shape[0]
    rows = back.shape[1] * back.shape[2]
    shape = (CX, CY, channels, NZ)
    return pl.pallas_call(
        decoder_kernel,
        out_shape=jax.ShapeDtypeStruct(shape, f32),
        in_specs=[smem, vmem, pl.BlockSpec(memory_space=pl.ANY)] + [vmem] * 3,
        out_specs=pl.BlockSpec(memory_space=pl.ANY),
        scratch_shapes=[
            pltpu.VMEM(back.shape, f32),
            pltpu.VMEM((back.shape[0], LANES // channels, rows, LANES), f32),
            pltpu.VMEM((CX * CY, channels, NZ), f32),
            pltpu.VMEM(shape, f32),
            pltpu.SemaphoreType.DMA((CX * CY * channels // LANES,)),
            pltpu.SemaphoreType.DMA,
        ],
        name="decoder",
    )(codes, held, back, inverse, w_point, b_point[None])


def local(
    features,
    offsets,
    point_cell,
    tile_owner,
    tile_local,
    live_count,
    w_first,
    b_first,
    w_second,
    b_second,
    w_third,
    w_point,
    b_point,
    w_modes,
):
    z_table, backward, lift, inverse = tables(
        lax.axis_size("gx"), lax.axis_size("gy"), w_modes.shape[0]
    )
    codes, held, back = encoder(
        features,
        offsets,
        point_cell,
        tile_owner,
        tile_local,
        live_count,
        w_first,
        b_first,
        w_second,
        b_second,
        w_third,
        w_modes,
        z_table,
        backward,
        lift,
    )
    return decoder(codes, held, back, inverse, w_point, b_point)


def solution(mesh):
    placed = (
        P(None, ("gx", "gy")),
        P(None, ("gx", "gy")),
        P(("gx", "gy")),
        P(("gx", "gy"), None),
        P(("gx", "gy"), None),
        P(("gx", "gy")),
        P(),
        P(),
        P(),
        P(),
        P(),
        P(),
        P(),
        P(None, "gx", "gy", None, None, None),
    )
    return jax.shard_map(
        local, mesh=mesh, in_specs=placed, out_specs=P("gx", "gy", None, None), check_vma=False
    )
```
